512 devices in a mesh: sample: 4 (over z_hi), gx: 8 (over z_lo, core), gy: 4 (over x), gz: 4 (over y).
Axes of the slice: x: 4, y: 4, z: 16 (z_hi: 4, z_lo: 4; z = z_hi * 4 + z_lo), core: 2. Of those that a mesh axis runs over, the one named last changes fastest.
Arguments:
- volume: bfloat16 [64, 64, 64, 128], P(('sample', 'gx'), 'gy', 'gz'), parts along dimension 0, may hold values from -6 to 6
- conv4_weight: bfloat16 [3, 3, 3, 128, 256], replicated, may hold values from -0.109375 to 0.109375
- conv5_weight: bfloat16 [3, 3, 3, 256, 512], P(None, None, None, None, ('gy', 'gz')), may hold values from -0.078125 to 0.078125
Outputs:
- features: bfloat16 [32, 32, 32, 512], P(('sample', 'gx'), None, None, ('gy', 'gz')), parts along dimension 0
The draws below stay inside these ranges and needn't reach their ends.
There are 4 independent parts, one for each index of `sample`. The reference program is written for one: setup_inputs(seed, part) draws one part's arguments, and reference() takes and returns one part's arrays. A program takes and returns all parts, laid end to end along the dimension named above; an argument that names none is the same for every part. Nothing has to cross between parts.
All inputs are finite; a program needn't handle non-finite values.
Results may differ from the reference program's by a relative error of at most 0.009.
Values may be sent and summed in bfloat16 or wider, within the bound.
A program may use at most 64 MiB of HBM per device.

```python
import jax
import jax.numpy as jnp
from jax import lax

CIN = 128
C4 = 256
C5 = 512
NX = 16
NY = 64
NZ = 64


def levels(rng, extent, cuts, least, top_value):
    loudness, own = 1.0, jax.random.fold_in(rng, 6)
    for axis_at, parts in cuts:
        steps = jnp.exp(jax.random.uniform(jax.random.fold_in(own, axis_at), (parts,), jnp.float32, least / len(cuts), top_value / len(cuts)))
        loudness = loudness * jnp.repeat(steps, extent[axis_at] // parts).reshape([-1 if axis == axis_at else 1 for axis in range(len(extent))])
    return loudness


def scatter_about(stream_key, extent, scale, limit, pieces=(), dtype=jnp.bfloat16):
    gain = levels(stream_key, extent, pieces, -0.22, 0.18) if pieces else 1.0
    entries = jax.random.normal(stream_key, extent, jnp.float32) * scale * gain
    return jnp.minimum(jnp.maximum(entries, -limit), limit).astype(dtype)


def setup_inputs(seed: int = 0, part: int = 0) -> dict:
    seeds = jax.random.split(jax.random.key(seed), 4)
    part_keys = jax.random.split(jax.random.fold_in(seeds[3], part), 4)
    volume = scatter_about(part_keys[0], (NX, NY, NZ, CIN), 1.0, 6.0, ((0, 8), (1, 4), (2, 4)))
    conv4_weight = scatter_about(seeds[1], (3, 3, 3, CIN, C4), (27 * CIN) ** -0.5, 0.109375)
    conv5_weight = scatter_about(seeds[2], (3, 3, 3, C4, C5), (27 * C4) ** -0.5, 0.078125, ((4, 16),))
    return dict(volume=volume, conv4_weight=conv4_weight, conv5_weight=conv5_weight)


def convolve(maps, kernel):
    result = lax.conv_general_dilated(maps.astype(jnp.float32)[None], kernel.astype(jnp.float32), (1, 1, 1), "SAME", dimension_numbers=("NDHWC", "DHWIO", "NDHWC"), precision=lax.Precision.HIGHEST)
    return result[0]


def reference(volume, conv4_weight, conv5_weight):
    hidden = convolve(volume, conv4_weight)
    leaked = jnp.where(hidden > 0, hidden, 0.3 * hidden)
    sizes = leaked.shape
    blocks = leaked.reshape(sizes[0] // 2, 2, sizes[1] // 2, 2, sizes[2] // 2, 2, sizes[3])
    pooled = jnp.max(blocks, axis=(1, 3, 5)).astype(jnp.bfloat16)
    return convolve(pooled, conv5_weight).astype(jnp.bfloat16)
```

```python
import functools

import jax
import jax.numpy as jnp
from jax import lax
from jax.experimental import pallas as pl
from jax.experimental.pallas import tpu as pltpu
from jax.sharding import PartitionSpec as P

MESH = pl.DeviceIdType.MESH
BF16, F32 = jnp.bfloat16, jnp.float32
CIN, C4, FILTERS = 128, 256, 32
PLANE = 32
SHIFTS = [(i, j, k) for i in (-1, 0, 1) for j in (-1, 0, 1) for k in (-1, 0, 1) if (i, j, k) != (0, 0, 0)]


def kernel(
    sizes, v, w4, w5, out,
    pad, wide, taps, w4b, w5b, zs, yz, zh, ch, pool, block, blocks, slab, edge, sent, got, packed,
    load_sem, halo_send, halo_recv, block_send, block_recv, part_send, part_recv,
):
    ngx, ngy, ngz = sizes
    g, a, b = lax.axis_index("gx"), lax.axis_index("gy"), lax.axis_index("gz")

    def there(dg, da, db):
        ok = None
        for at, step, n in ((g, dg, ngx), (a, da, ngy), (b, db, ngz)):
            if step:
                fine = (at > 0) if step < 0 else (at < n - 1)
                ok = fine if ok is None else jnp.logical_and(ok, fine)
        return ok

    def device(dg, da, db):
        return {"gx": g + dg, "gy": a + da, "gz": b + db}

    own_load = pltpu.make_async_copy(v, pad.at[1:3, 1:17], load_sem.at[0])
    own_load.start()
    w4_load = pltpu.make_async_copy(w4, w4b, load_sem.at[1])
    w4_load.start()
    w5_loads = []
    for dx in range(3):
        for dy in range(3):
            w5_loads.append(
                pltpu.make_async_copy(
                    w5.at[dx, dy],
                    w5b.at[:, dx * FILTERS : (dx + 1) * FILTERS, dy * C4 : (dy + 1) * C4],
                    load_sem.at[2 + dx * 3 + dy],
                )
            )
    for load in w5_loads:
        load.start()

    barrier = pltpu.get_barrier_semaphore()
    for da in range(ngy):
        for db in range(ngz):
            if (da, db) != (0, 0):
                pl.semaphore_signal(
                    barrier, inc=1, device_id={"gy": lax.rem(a + da, ngy), "gz": lax.rem(b + db, ngz)}, device_id_type=MESH
                )
    for shift in SHIFTS:
        if shift[0]:
            @pl.when(there(*shift))
            def _():
                pl.semaphore_signal(barrier, inc=1, device_id=device(*shift), device_id_type=MESH)

    def near(at, n):
        return jnp.int32(1) + (at > 0).astype(jnp.int32) + (at < n - 1).astype(jnp.int32)

    greeted = (near(g, ngx) - 1) * near(a, ngy) * near(b, ngz) + (ngy * ngz - 1)

    @pl.when(g == 0)
    def _():
        pad[0] = jnp.zeros(pad.shape[1:], BF16)
        zh[:, 0] = jnp.zeros((2, 16, CIN), BF16)
        ch[:, :, 0] = jnp.zeros((2, 2, 8, CIN), F32)

    @pl.when(g == ngx - 1)
    def _():
        pad[3] = jnp.zeros(pad.shape[1:], BF16)
        zh[:, 3] = jnp.zeros((2, 16, CIN), BF16)
        ch[:, :, 2] = jnp.zeros((2, 2, 8, CIN), F32)

    for side, edge_at in ((0, 0), (1, ngy - 1)):
        @pl.when(a == edge_at)
        def _():
            pad[:, 17 * side] = jnp.zeros((4, 16, CIN), BF16)
            ch[:, side] = jnp.zeros((2, 3, 8, CIN), F32)

    for side, edge_at in ((0, 0), (1, ngz - 1)):
        @pl.when(b == edge_at)
        def _():
            zh[side] = jnp.zeros((4, 16, CIN), BF16)
            ch[side] = jnp.zeros((2, 3, 8, CIN), F32)

    slab[0] = jnp.zeros((PLANE, C4), BF16)
    slab[PLANE + 1] = jnp.zeros((PLANE, C4), BF16)
    w5b[:, 96:128, :] = jnp.zeros((3, 32, 3 * C4), BF16)
    edge[:, :, 0:8] = jnp.zeros((2, 8, 8, 128), F32)
    edge[:, :, 40:48] = jnp.zeros((2, 8, 8, 128), F32)
    yz[...] = jnp.zeros(yz.shape, F32)

    own_load.wait()
    for x in (1, 2):
        for y in range(1, 17):
            row = (x * 18 + y) * 32 + 8
            wide[row : row + 16, :] = pad[x, y].astype(F32)
    for side, z in ((0, 0), (1, 15)):
        for x in (0, 1):
            first = ((x + 1) * 18 + 1) * 32 + 8 + z
            column = wide[pl.ds(first, 16, stride=32), :]
            zs[side, x] = column.astype(BF16)
            for ys, y in ((0, 0), (1, 15)):
                yz[side, ys, x : x + 1, :] = column[y : y + 1]

    pl.semaphore_wait(barrier, greeted)

    def halo(shift):
        dg, da, db = shift
        x = {-1: 0, 1: 1}.get(dg)
        px = {-1: 3, 1: 0}.get(dg)
        y = {-1: 0, 1: 15}.get(da)
        py = {-1: 17, 1: 0}.get(da)
        s = {-1: 0, 1: 1}.get(db)
        if db == 0:
            if da == 0:
                src, dst = pad.at[x + 1, 1:17], pad.at[px, 1:17]
            elif dg == 0:
                src, dst = pad.at[1:3, y + 1], pad.at[1:3, py]
            else:
                src, dst = pad.at[x + 1, y + 1], pad.at[px, py]
        elif da == 0:
            if dg == 0:
                src, dst = zs.at[s], zh.at[1 - s, 1:3]
            else:
                src, dst = zs.at[s, x], zh.at[1 - s, px]
        else:
            ys = {-1: 0, 1: 1}[da]
            src, dst = yz.at[s, ys], ch.at[1 - s, 1 - ys, {-1: 2, 0: 1, 1: 0}[dg]]
        number = SHIFTS.index(shift)
        return pltpu.make_async_remote_copy(
            src_ref=src, dst_ref=dst, send_sem=halo_send.at[number], recv_sem=halo_recv.at[number],
            device_id=device(*shift), device_id_type=MESH,
        )

    for shift in SHIFTS:
        @pl.when(there(*shift))
        def _():
            halo(shift).start()
    for shift in SHIFTS:
        @pl.when(there(*(-i for i in shift)))
        def _():
            halo(shift).wait_recv()

    for x in range(4):
        for y in range(18):
            if not (x in (1, 2) and 1 <= y <= 16):
                row = (x * 18 + y) * 32 + 8
                wide[row : row + 16, :] = pad[x, y].astype(F32)
        for side, at in ((0, 7), (1, 24)):
            wide[pl.ds((x * 18 + 1) * 32 + at, 16, stride=32), :] = zh[side, x].astype(F32)
            for ys, y in ((0, 0), (1, 17)):
                source, row = ((0, 1), (1, 0), (1, 1), (2, 0))[x]
                first = (x * 18 + y) * 32 + at
                wide[first : first + 1, :] = ch[side, ys, source, row : row + 1, :]
    for x in range(4):
        for y in range(18):
            row = (x * 18 + y) * 32
            left = wide[row + 7 : row + 23, :].astype(BF16)
            right = wide[row + 9 : row + 25, :].astype(BF16)
            taps[x, y * 16 : y * 16 + 16, :] = jnp.concatenate([left, pad[x, y], right], axis=-1)

    w4_load.wait()
    for part in range(4):
        tops = None
        for x in (0, 1):
            lhs = jnp.concatenate(
                [taps[x + dx, (4 * part + dy) * 16 : (4 * part + dy) * 16 + 64, :] for dx in range(3) for dy in range(3)], axis=-1
            )
            hidden = jnp.dot(lhs, w4b[...], preferred_element_type=F32)
            tops = hidden if tops is None else jnp.maximum(tops, hidden)
        tops = jnp.max(tops.reshape(2, 2, 16, C4), axis=1).reshape(32, C4)
        for half in range(2):
            pool[half, part * 32 : part * 32 + 32, :] = tops[:, half * 128 : half * 128 + 128]
    for half in range(2):
        tops = jnp.maximum(pool[half, pl.ds(0, 64, stride=2), :], pool[half, pl.ds(1, 64, stride=2), :])
        block[:, half * 128 : half * 128 + 128] = jnp.where(tops > 0, tops, 0.3 * tops).astype(BF16)

    me = a * ngz + b
    offsets = [(da, db) for da in range(ngy) for db in range(ngz) if (da, db) != (0, 0)]

    def spread(da, db):
        number = da * ngz + db
        return pltpu.make_async_remote_copy(
            src_ref=block, dst_ref=blocks.at[me], send_sem=block_send.at[number], recv_sem=block_recv.at[number],
            device_id={"gy": lax.rem(a + da, ngy), "gz": lax.rem(b + db, ngz)}, device_id_type=MESH,
        )

    for da, db in offsets:
        spread(da, db).start()
    blocks[me] = block[...]
    for load in w5_loads:
        load.wait()
    for da, db in offsets:
        spread(da, db).wait_recv()

    for row in range(ngy):
        for pair in range(2):
            halves = [blocks[row * ngz + 2 * pair + i].astype(F32).reshape(8, 1, 8, C4) for i in range(2)]
            tile = jnp.concatenate(halves, axis=1).reshape(8, 16, C4).astype(BF16)
            slab[1 + 8 * row : 9 + 8 * row, 16 * pair : 16 * pair + 16, :] = tile

    def part_copy(q, k):
        dg = 1 if k == 0 else -1
        return pltpu.make_async_remote_copy(
            src_ref=sent.at[k, q], dst_ref=got.at[k, q], send_sem=part_send.at[k, q], recv_sem=part_recv.at[k, q],
            device_id={"gx": g + dg}, device_id_type=MESH,
        )

    lane = lax.broadcasted_iota(jnp.int32, (64, 128), 1)

    def group(rows, k):
        moved = [
            rows[64 * u : 64 * u + 64] if u == k else pltpu.roll(rows[64 * u : 64 * u + 64], (32 * (u - k)) % 128, axis=1)
            for u in range(4)
        ]
        return jnp.where(lane < 64, jnp.where(lane < 32, moved[0], moved[1]), jnp.where(lane < 96, moved[2], moved[3]))

    for q in range(4):
        lhs = jnp.concatenate([slab[8 * q + dy : 8 * q + dy + 8].reshape(256, C4) for dy in range(3)], axis=-1)
        sums = [
            lax.dot_general(lhs, w5b[dz], (((1,), (1,)), ((), ())), preferred_element_type=F32).reshape(8, PLANE, 128)
            for dz in range(3)
        ]
        edge[0, :, 8:40] = sums[0]
        edge[1, :, 8:40] = sums[2]
        total = (sums[1] + edge[0, :, 7:39] + edge[1, :, 9:41]).reshape(256, 128)
        sent[0, q] = group(total, 0).astype(BF16)
        sent[1, q] = group(total, 2).astype(BF16)

        @pl.when(g < ngx - 1)
        def _():
            part_copy(q, 0).start()

        @pl.when(g > 0)
        def _():
            part_copy(q, 1).start()

        packed[q] = group(total, 1)

    @pl.when(g > 0)
    def _():
        for q in range(4):
            part_copy(q, 0).wait_recv()
            packed[q] += got[0, q].astype(F32)

    @pl.when(g < ngx - 1)
    def _():
        for q in range(4):
            part_copy(q, 1).wait_recv()
            packed[q] += got[1, q].astype(F32)

    out[...] = packed[...].astype(BF16)

    for shift in SHIFTS:
        @pl.when(there(*shift))
        def _():
            halo(shift).wait_send()
    for da, db in offsets:
        spread(da, db).wait_send()

    @pl.when(g < ngx - 1)
    def _():
        for q in range(4):
            part_copy(q, 0).wait_send()

    @pl.when(g > 0)
    def _():
        for q in range(4):
            part_copy(q, 1).wait_send()


def body(sizes, volume, conv4_weight, conv5_weight):
    ngx, ngy, ngz = sizes
    any_space = pl.BlockSpec(memory_space=pl.ANY)
    packed = pl.pallas_call(
        functools.partial(kernel, sizes),
        out_shape=jax.ShapeDtypeStruct((4, 64, 128), BF16),
        in_specs=[any_space] * 3,
        out_specs=pl.BlockSpec(memory_space=pltpu.VMEM),
        scratch_shapes=[
            pltpu.VMEM((4, 18, 16, CIN), BF16),
            pltpu.VMEM((4 * 18 * 32, CIN), F32),
            pltpu.VMEM((4, 18 * 16, 3 * CIN), BF16),
            pltpu.VMEM((27 * CIN, C4), BF16),
            pltpu.VMEM((3, 128, 3 * C4), BF16),
            pltpu.VMEM((2, 2, 16, CIN), BF16),
            pltpu.VMEM((2, 2, 8, CIN), F32),
            pltpu.VMEM((2, 4, 16, CIN), BF16),
            pltpu.VMEM((2, 2, 3, 8, CIN), F32),
            pltpu.VMEM((2, 128, 128), F32),
            pltpu.VMEM((64, C4), BF16),
            pltpu.VMEM((ngy * ngz, 64, C4), BF16),
            pltpu.VMEM((PLANE + 2, PLANE, C4), BF16),
            pltpu.VMEM((2, 8, 48, 128), F32),
            pltpu.VMEM((2, 4, 64, 128), BF16),
            pltpu.VMEM((2, 4, 64, 128), BF16),
            pltpu.VMEM((4, 64, 128), F32),
            pltpu.SemaphoreType.DMA((11,)),
            pltpu.SemaphoreType.DMA((26,)),
            pltpu.SemaphoreType.DMA((26,)),
            pltpu.SemaphoreType.DMA((ngy * ngz,)),
            pltpu.SemaphoreType.DMA((ngy * ngz,)),
            pltpu.SemaphoreType.DMA((2, 4)),
            pltpu.SemaphoreType.DMA((2, 4)),
        ],
        compiler_params=pltpu.CompilerParams(
            collective_id=0, has_side_effects=True, vmem_limit_bytes=40 * 1024 * 1024
        ),
    )(
        volume,
        conv4_weight.reshape(27 * CIN, C4),
        jnp.swapaxes(conv5_weight, 3, 4),
    )
    cells = packed.reshape(4, 2, PLANE, 4, FILTERS).transpose(0, 3, 1, 2, 4)
    return cells.reshape(1, PLANE, PLANE, FILTERS)


def solution(mesh):
    sizes = (mesh.shape["gx"], mesh.shape["gy"], mesh.shape["gz"])
    return jax.shard_map(
        functools.partial(body, sizes),
        mesh=mesh,
        in_specs=(
            P(("sample", "gx"), "gy", "gz", None),
            P(),
            P(None, None, None, None, ("gy", "gz")),
        ),
        out_specs=P(("sample", "gx"), None, None, ("gy", "gz")),
        check_vma=False,
    )
```

```python
import functools

import jax
import jax.numpy as jnp
from jax import lax
from jax.experimental import pallas as pl
from jax.experimental.pallas import tpu as pltpu
from jax.sharding import PartitionSpec as P

MESH = pl.DeviceIdType.MESH
BF16, F32 = jnp.bfloat16, jnp.float32
CIN, C4, FILTERS = 128, 256, 32
PLANE = 32
SHIFTS = [(i, j, k) for i in (-1, 0, 1) for j in (-1, 0, 1) for k in (-1, 0, 1) if (i, j, k) != (0, 0, 0)]


def kernel(
    sizes, v, w4, w5, out,
    pad, wide, taps, w4b, w5b, zs, yz, zh, ch, pool, block, blocks, rim, rims, slab, edge, sent, got, packed,
    load_sem, halo_send, halo_recv, block_send, block_recv, rim_send, rim_recv, part_send, part_recv, shard_send, shard_recv,
):
    ngx, ngy, ngz = sizes
    g, a, b = lax.axis_index("gx"), lax.axis_index("gy"), lax.axis_index("gz")
    half = lax.div(a, 2)
    core = lax.rem(g, 2)
    other = ngy - 1 - a
    beside = 4 * half + 1 - a

    def there(dg, da, db):
        ok = None
        for at, step, n in ((g, dg, ngx), (a, da, ngy), (b, db, ngz)):
            if step:
                fine = (at > 0) if step < 0 else (at < n - 1)
                ok = fine if ok is None else jnp.logical_and(ok, fine)
        return ok

    def device(dg, da, db):
        return {"gx": g + dg, "gy": a + da, "gz": b + db}

    own_load = pltpu.make_async_copy(v, pad.at[1:3, 1:17], load_sem.at[0])
    own_load.start()
    w4_load = pltpu.make_async_copy(w4, w4b, load_sem.at[1])
    w4_load.start()
    w5_loads = []
    for dx in range(3):
        for dy in range(3):
            w5_loads.append(
                pltpu.make_async_copy(
                    w5.at[dx, dy],
                    w5b.at[:, dx * FILTERS : (dx + 1) * FILTERS, dy * C4 : (dy + 1) * C4],
                    load_sem.at[2 + dx * 3 + dy],
                )
            )
    for load in w5_loads:
        load.start()

    def finish(stage):
        if stage < 3:
            w4_load.wait()
        if stage < 2:
            for load in w5_loads:
                load.wait()
        if stage >= 2:
            for shift in SHIFTS:
                @pl.when(there(*shift))
                def _():
                    halo(shift).wait_send()
        if stage >= 2:
            shard_copy().wait_send()
            if stage < 4:
                shard_copy().wait_recv()
        if stage >= 4:
            shard_relay().wait_send()
            for di, db in offsets:
                spread(di, db).wait_send()

            @pl.when(jnp.logical_or(a == 1, a == 2))
            def _():
                for t in range(2):
                    for db in range(ngz):
                        rim_copy(t, db).wait_send()
        if stage >= 5:
            for p, k in parts:
                @part_when(k, True)
                def _():
                    for q in range(2):
                        part_copy(p, k, q).wait_send()

    barrier = pltpu.get_barrier_semaphore()
    for da in range(ngy):
        for db in range(ngz):
            if (da, db) != (0, 0):
                pl.semaphore_signal(
                    barrier, inc=1, device_id={"gy": lax.rem(a + da, ngy), "gz": lax.rem(b + db, ngz)}, device_id_type=MESH
                )
    for shift in SHIFTS:
        if shift[0]:
            @pl.when(there(*shift))
            def _():
                pl.semaphore_signal(barrier, inc=1, device_id=device(*shift), device_id_type=MESH)

    outer = jnp.logical_or(a == 0, a == ngy - 1)
    for dg in (-1, 1):
        @pl.when(jnp.logical_and(there(dg, 0, 0), outer))
        def _():
            pl.semaphore_signal(barrier, inc=1, device_id={"gx": g + dg, "gy": other}, device_id_type=MESH)

    def near(at, n):
        return jnp.int32(1) + (at > 0).astype(jnp.int32) + (at < n - 1).astype(jnp.int32)

    greeted = (near(g, ngx) - 1) * (near(a, ngy) * near(b, ngz) + outer.astype(jnp.int32)) + (ngy * ngz - 1)

    @pl.when(g == 0)
    def _():
        pad[0] = jnp.zeros(pad.shape[1:], BF16)
        zh[:, 0] = jnp.zeros((2, 16, CIN), BF16)
        ch[:, :, 0] = jnp.zeros((2, 2, 8, CIN), F32)

    @pl.when(g == ngx - 1)
    def _():
        pad[3] = jnp.zeros(pad.shape[1:], BF16)
        zh[:, 3] = jnp.zeros((2, 16, CIN), BF16)
        ch[:, :, 2] = jnp.zeros((2, 2, 8, CIN), F32)

    for side, edge_at in ((0, 0), (1, ngy - 1)):
        @pl.when(a == edge_at)
        def _():
            pad[:, 17 * side] = jnp.zeros((4, 16, CIN), BF16)
            ch[:, side] = jnp.zeros((2, 3, 8, CIN), F32)

    for side, edge_at in ((0, 0), (1, ngz - 1)):
        @pl.when(b == edge_at)
        def _():
            zh[side] = jnp.zeros((4, 16, CIN), BF16)
            ch[side] = jnp.zeros((2, 3, 8, CIN), F32)

    slab[17 * half] = jnp.zeros((PLANE, C4), BF16)
    w5b[:, 192:256, :] = jnp.zeros((3, 64, 3 * C4), BF16)
    edge[:, :, 0:8] = jnp.zeros((2, 8, 8, 256), F32)
    edge[:, :, 40:48] = jnp.zeros((2, 8, 8, 256), F32)
    yz[...] = jnp.zeros(yz.shape, F32)

    own_load.wait()
    for x in (1, 2):
        for y in range(1, 17):
            row = (x * 18 + y) * 32 + 8
            wide[row : row + 16, :] = pad[x, y].astype(F32)
    for side, z in ((0, 0), (1, 15)):
        for x in (0, 1):
            first = ((x + 1) * 18 + 1) * 32 + 8 + z
            column = wide[pl.ds(first, 16, stride=32), :]
            zs[side, x] = column.astype(BF16)
            for ys, y in ((0, 0), (1, 15)):
                yz[side, ys, x : x + 1, :] = column[y : y + 1]

    pl.semaphore_wait(barrier, greeted)

    def halo(shift):
        dg, da, db = shift
        x = {-1: 0, 1: 1}.get(dg)
        px = {-1: 3, 1: 0}.get(dg)
        y = {-1: 0, 1: 15}.get(da)
        py = {-1: 17, 1: 0}.get(da)
        s = {-1: 0, 1: 1}.get(db)
        if db == 0:
            if da == 0:
                src, dst = pad.at[x + 1, 1:17], pad.at[px, 1:17]
            elif dg == 0:
                src, dst = pad.at[1:3, y + 1], pad.at[1:3, py]
            else:
                src, dst = pad.at[x + 1, y + 1], pad.at[px, py]
        elif da == 0:
            if dg == 0:
                src, dst = zs.at[s], zh.at[1 - s, 1:3]
            else:
                src, dst = zs.at[s, x], zh.at[1 - s, px]
        else:
            ys = {-1: 0, 1: 1}[da]
            src, dst = yz.at[s, ys], ch.at[1 - s, 1 - ys, {-1: 2, 0: 1, 1: 0}[dg]]
        number = SHIFTS.index(shift)
        return pltpu.make_async_remote_copy(
            src_ref=src, dst_ref=dst, send_sem=halo_send.at[number], recv_sem=halo_recv.at[number],
            device_id=device(*shift), device_id_type=MESH,
        )

    for shift in SHIFTS:
        @pl.when(there(*shift))
        def _():
            halo(shift).start()

    def shard_rows(first, which):
        return w5b.at[:, pl.ds(pl.multiple_of(first + 48 * which, 16), 48), :]

    def shard_copy():
        return pltpu.make_async_remote_copy(
            src_ref=shard_rows(0, core), dst_ref=shard_rows(96, core), send_sem=shard_send.at[0], recv_sem=shard_recv.at[0],
            device_id={"gy": other}, device_id_type=MESH,
        )

    def shard_relay():
        return pltpu.make_async_remote_copy(
            src_ref=shard_rows(96, core), dst_ref=shard_rows(96, core), send_sem=shard_send.at[1], recv_sem=shard_recv.at[1],
            device_id={"gx": g + 1 - 2 * core}, device_id_type=MESH,
        )

    for load in w5_loads:
        load.wait()
    shard_copy().start()

    for shift in SHIFTS:
        @pl.when(there(*(-i for i in shift)))
        def _():
            halo(shift).wait_recv()

    for x in range(4):
        for y in range(18):
            if not (x in (1, 2) and 1 <= y <= 16):
                row = (x * 18 + y) * 32 + 8
                wide[row : row + 16, :] = pad[x, y].astype(F32)
        for side, at in ((0, 7), (1, 24)):
            wide[pl.ds((x * 18 + 1) * 32 + at, 16, stride=32), :] = zh[side, x].astype(F32)
            for ys, y in ((0, 0), (1, 17)):
                source, row = ((0, 1), (1, 0), (1, 1), (2, 0))[x]
                first = (x * 18 + y) * 32 + at
                wide[first : first + 1, :] = ch[side, ys, source, row : row + 1, :]
    for x in range(4):
        for y in range(18):
            row = (x * 18 + y) * 32
            left = wide[row + 7 : row + 23, :].astype(BF16)
            right = wide[row + 9 : row + 25, :].astype(BF16)
            taps[x, y * 16 : y * 16 + 16, :] = jnp.concatenate([left, pad[x, y], right], axis=-1)

    w4_load.wait()
    for part in range(4):
        tops = None
        for x in (0, 1):
            lhs = jnp.concatenate(
                [taps[x + dx, (4 * part + dy) * 16 : (4 * part + dy) * 16 + 64, :] for dx in range(3) for dy in range(3)], axis=-1
            )
            hidden = jnp.dot(lhs, w4b[...], preferred_element_type=F32)
            tops = hidden if tops is None else jnp.maximum(tops, hidden)
        tops = jnp.max(tops.reshape(2, 2, 16, C4), axis=1).reshape(32, C4)
        for lanes in range(2):
            pool[lanes, part * 32 : part * 32 + 32, :] = tops[:, lanes * 128 : lanes * 128 + 128]
    for lanes in range(2):
        tops = jnp.maximum(pool[lanes, pl.ds(0, 64, stride=2), :], pool[lanes, pl.ds(1, 64, stride=2), :])
        block[:, lanes * 128 : lanes * 128 + 128] = jnp.where(tops > 0, tops, 0.3 * tops).astype(BF16)

    mine = (a - 2 * half) * ngz + b
    offsets = [(di, db) for di in range(2) for db in range(ngz) if (di, db) != (0, 0)]

    def spread(di, db):
        number = di * ngz + db
        return pltpu.make_async_remote_copy(
            src_ref=block, dst_ref=blocks.at[mine], send_sem=block_send.at[number], recv_sem=block_recv.at[number],
            device_id={"gy": beside if di else a, "gz": lax.rem(b + db, ngz)}, device_id_type=MESH,
        )

    def rim_copy(t, db):
        return pltpu.make_async_remote_copy(
            src_ref=rim, dst_ref=rims.at[b], send_sem=rim_send.at[t, db], recv_sem=rim_recv.at[db],
            device_id={"gy": 2 * (1 - half) + t, "gz": lax.rem(b + db, ngz)}, device_id_type=MESH,
        )

    for at, first in ((1, 56), (2, 0)):
        @pl.when(a == at)
        def _():
            rim[...] = block[first : first + 8, :].astype(F32)

    for di, db in offsets:
        spread(di, db).start()

    @pl.when(jnp.logical_or(a == 1, a == 2))
    def _():
        for t in range(2):
            for db in range(ngz):
                rim_copy(t, db).start()

    blocks[mine] = block[...]
    shard_copy().wait_recv()
    shard_relay().start()
    for di, db in offsets:
        spread(di, db).wait_recv()
    for db in range(ngz):
        rim_copy(0, db).wait_recv()
    shard_relay().wait_recv()

    for row in range(2):
        for pair in range(2):
            halves = [blocks[row * ngz + 2 * pair + i].astype(F32).reshape(8, 1, 8, C4) for i in range(2)]
            tile = jnp.concatenate(halves, axis=1).reshape(8, 16, C4).astype(BF16)
            slab[1 + 8 * row : 9 + 8 * row, 16 * pair : 16 * pair + 16, :] = tile
    slab[17 * (1 - half)] = rims[...].reshape(PLANE, C4).astype(BF16)

    parts = [(p, k) for p in range(2) for k in range(3) if (p, k) != (0, 1)]

    def part_when(k, sender):
        if k == 1:
            return lambda f: f()
        if (k == 0) == sender:
            return pl.when(g < ngx - 1)
        return pl.when(g > 0)

    def part_copy(p, k, q):
        return pltpu.make_async_remote_copy(
            src_ref=sent.at[p, k, q], dst_ref=got.at[p, k, q], send_sem=part_send.at[p, k, q], recv_sem=part_recv.at[p, k, q],
            device_id={"gx": g + 1 - k, "gy": other if p else a}, device_id_type=MESH,
        )

    lane = lax.broadcasted_iota(jnp.int32, (64, 128), 1)

    def group(rows, j):
        tile, k = divmod(j, 4)
        moved = [
            pltpu.roll(rows[64 * u : 64 * u + 64, 128 * tile : 128 * tile + 128], (32 * (u - k)) % 128, axis=1)
            if u != k else rows[64 * u : 64 * u + 64, 128 * tile : 128 * tile + 128]
            for u in range(4)
        ]
        return jnp.where(lane < 64, jnp.where(lane < 32, moved[0], moved[1]), jnp.where(lane < 96, moved[2], moved[3]))

    for q in range(2):
        lhs = jnp.concatenate([slab[8 * q + dy : 8 * q + dy + 8].reshape(256, C4) for dy in range(3)], axis=-1)
        sums = [
            lax.dot_general(lhs, w5b[dz], (((1,), (1,)), ((), ())), preferred_element_type=F32).reshape(8, PLANE, 256)
            for dz in range(3)
        ]
        edge[0, :, 8:40] = sums[0]
        edge[1, :, 8:40] = sums[2]
        total = (sums[1] + edge[0, :, 7:39] + edge[1, :, 9:41]).reshape(256, 256)
        for p, k in parts:
            sent[p, k, q] = group(total, 3 * p + k).astype(BF16)

            @part_when(k, True)
            def _():
                part_copy(p, k, q).start()

        packed[0, q] = group(total, 1)

    for q in range(2):
        part_copy(1, 1, q).wait_recv()
        packed[1, q] = got[1, 1, q].astype(F32)
    for k in (0, 2):
        @part_when(k, False)
        def _():
            for p in range(2):
                for q in range(2):
                    part_copy(p, k, q).wait_recv()
                    packed[p, q] += got[p, k, q].astype(F32)

    out[half] = packed[0].astype(BF16)
    out[1 - half] = packed[1].astype(BF16)

    finish(9)


def body(sizes, volume, conv4_weight, conv5_weight):
    ngx, ngy, ngz = sizes
    any_space = pl.BlockSpec(memory_space=pl.ANY)
    packed = pl.pallas_call(
        functools.partial(kernel, sizes),
        out_shape=jax.ShapeDtypeStruct((2, 2, 64, 128), BF16),
        in_specs=[any_space] * 3,
        out_specs=pl.BlockSpec(memory_space=pltpu.VMEM),
        scratch_shapes=[
            pltpu.VMEM((4, 18, 16, CIN), BF16),
            pltpu.VMEM((4 * 18 * 32, CIN), F32),
            pltpu.VMEM((4, 18 * 16, 3 * CIN), BF16),
            pltpu.VMEM((27 * CIN, C4), BF16),
            pltpu.VMEM((3, 256, 3 * C4), BF16),
            pltpu.VMEM((2, 2, 16, CIN), BF16),
            pltpu.VMEM((2, 2, 8, CIN), F32),
            pltpu.VMEM((2, 4, 16, CIN), BF16),
            pltpu.VMEM((2, 2, 3, 8, CIN), F32),
            pltpu.VMEM((2, 128, 128), F32),
            pltpu.VMEM((64, C4), BF16),
            pltpu.VMEM((2 * ngz, 64, C4), BF16),
            pltpu.VMEM((8, C4), F32),
            pltpu.VMEM((ngz, 8, C4), F32),
            pltpu.VMEM((18, PLANE, C4), BF16),
            pltpu.VMEM((2, 8, 48, 256), F32),
            pltpu.VMEM((2, 3, 2, 64, 128), BF16),
            pltpu.VMEM((2, 3, 2, 64, 128), BF16),
            pltpu.VMEM((2, 2, 64, 128), F32),
            pltpu.SemaphoreType.DMA((11,)),
            pltpu.SemaphoreType.DMA((26,)),
            pltpu.SemaphoreType.DMA((26,)),
            pltpu.SemaphoreType.DMA((2 * ngz,)),
            pltpu.SemaphoreType.DMA((2 * ngz,)),
            pltpu.SemaphoreType.DMA((2, ngz)),
            pltpu.SemaphoreType.DMA((ngz,)),
            pltpu.SemaphoreType.DMA((2, 3, 2)),
            pltpu.SemaphoreType.DMA((2, 3, 2)),
            pltpu.SemaphoreType.DMA((2,)),
            pltpu.SemaphoreType.DMA((2,)),
        ],
        compiler_params=pltpu.CompilerParams(
            collective_id=0, has_side_effects=True, vmem_limit_bytes=40 * 1024 * 1024
        ),
    )(
        *(pltpu.with_memory_space_constraint(x, pltpu.HBM) for x in (volume, conv4_weight.reshape(27 * CIN, C4), jnp.swapaxes(conv5_weight, 3, 4))),
    )
    cells = packed.reshape(4, 2, PLANE, 4, FILTERS).transpose(0, 3, 1, 2, 4)
    return cells.reshape(1, PLANE, PLANE, FILTERS)


def solution(mesh):
    sizes = (mesh.shape["gx"], mesh.shape["gy"], mesh.shape["gz"])
    return jax.shard_map(
        functools.partial(body, sizes),
        mesh=mesh,
        in_specs=(
            P(("sample", "gx"), "gy", "gz", None),
            P(),
            P(None, None, None, None, ("gy", "gz")),
        ),
        out_specs=P(("sample", "gx"), None, None, ("gy", "gz")),
        check_vma=False,
    )
```

```python
import functools

import jax
import jax.numpy as jnp
from jax import lax
from jax.experimental import pallas as pl
from jax.experimental.pallas import tpu as pltpu
from jax.sharding import PartitionSpec as P

MESH = pl.DeviceIdType.MESH
BF16, F32 = jnp.bfloat16, jnp.float32
CIN, C4, FILTERS = 128, 256, 32
PLANE = 32
SHIFTS = [(i, j, k) for i in (-1, 0, 1) for j in (-1, 0, 1) for k in (-1, 0, 1) if (i, j, k) != (0, 0, 0)]


def kernel(
    sizes, v, w4, w5, out,
    pad, wide, taps, w4b, w5b, zs, yz, zh, ch, hidden, pool, block, blocks, rim, rims, slab, broad, sent, got, packed,
    load_sem, halo_send, halo_recv, block_send, block_recv, rim_send, rim_recv, part_send, part_recv, shard_send, shard_recv,
):
    ngx, ngy, ngz = sizes
    g, a, b = lax.axis_index("gx"), lax.axis_index("gy"), lax.axis_index("gz")
    half = lax.div(a, 2)
    core = lax.rem(g, 2)
    other = ngy - 1 - a
    beside = 4 * half + 1 - a

    def there(dg, da, db):
        ok = None
        for at, step, n in ((g, dg, ngx), (a, da, ngy), (b, db, ngz)):
            if step:
                fine = (at > 0) if step < 0 else (at < n - 1)
                ok = fine if ok is None else jnp.logical_and(ok, fine)
        return ok

    def device(dg, da, db):
        return {"gx": g + dg, "gy": a + da, "gz": b + db}

    barrier = pltpu.get_barrier_semaphore()
    ring = sorted(SHIFTS, key=lambda shift: -sum(map(abs, shift)))
    for dg, da, db in ring:
        def greet():
            pl.semaphore_signal(
                barrier, inc=1,
                device_id={"gx": g + dg, "gy": lax.rem(a + da + ngy, ngy), "gz": lax.rem(b + db + ngz, ngz)},
                device_id_type=MESH,
            )
        if dg:
            pl.when(there(dg, 0, 0))(greet)
        else:
            greet()
    sides = (g > 0).astype(jnp.int32) + (g < ngx - 1).astype(jnp.int32)
    greeted = 9 * sides + 8

    own_load = pltpu.make_async_copy(v, pad.at[1:3, 1:17], load_sem.at[0])
    own_load.start()
    w4_load = pltpu.make_async_copy(w4, w4b, load_sem.at[1])
    w4_load.start()
    w5_loads = [
        pltpu.make_async_copy(
            w5.at[dx, dy, dz],
            w5b.at[dx * FILTERS : (dx + 1) * FILTERS, (3 * dz + dy) * C4 : (3 * dz + dy + 1) * C4],
            load_sem.at[2 + (dx * 3 + dy) * 3 + dz],
        )
        for dx in range(3)
        for dy in range(3)
        for dz in range(3)
    ]
    for load in w5_loads:
        load.start()

    def finish(stage):
        if stage < 2:
            w4_load.wait()
        if stage < 2:
            for load in w5_loads:
                load.wait()
        if stage == 2:
            halo_wait([shift for shift in SHIFTS if shift[0]])
            w4_load.wait()
        if 2 <= stage < 4:
            halo_sent()
            shard_copy().wait_send()
            shard_copy().wait_recv()
        if stage == 4:
            spread_sent()
        if stage >= 5:
            for p, k in parts:
                @part_when(k, True)
                def _():
                    for q in range(2):
                        part_copy(p, k, q).wait_send()

    @pl.when(g == 0)
    def _():
        pad[0] = jnp.zeros(pad.shape[1:], BF16)
        zh[:, 0] = jnp.zeros((2, 16, CIN), BF16)
        ch[:, :, 0] = jnp.zeros((2, 2, 8, CIN), F32)

    @pl.when(g == ngx - 1)
    def _():
        pad[3] = jnp.zeros(pad.shape[1:], BF16)
        zh[:, 3] = jnp.zeros((2, 16, CIN), BF16)
        ch[:, :, 2] = jnp.zeros((2, 2, 8, CIN), F32)

    for side, edge_at in ((0, 0), (1, ngy - 1)):
        @pl.when(a == edge_at)
        def _():
            pad[:, 17 * side] = jnp.zeros((4, 16, CIN), BF16)
            ch[:, side] = jnp.zeros((2, 3, 8, CIN), F32)

    for side, edge_at in ((0, 0), (1, ngz - 1)):
        @pl.when(b == edge_at)
        def _():
            zh[side] = jnp.zeros((4, 16, CIN), BF16)
            ch[side] = jnp.zeros((2, 3, 8, CIN), F32)

    for dz in range(3):
        slab[dz, 17 * half] = jnp.zeros((PLANE, C4), BF16)
    w5b[192:256, :] = jnp.zeros((64, 9 * C4), BF16)
    broad[:, 0:8] = jnp.zeros((18, 8, C4), F32)
    broad[:, 40:48] = jnp.zeros((18, 8, C4), F32)
    yz[...] = jnp.zeros(yz.shape, F32)

    own_load.wait()
    for x in (1, 2):
        for y in range(1, 17):
            row = (x * 18 + y) * 32 + 8
            wide[row : row + 16, :] = pad[x, y].astype(F32)
    for side, z in ((0, 0), (1, 15)):
        for x in (0, 1):
            first = ((x + 1) * 18 + 1) * 32 + 8 + z
            column = wide[pl.ds(first, 16, stride=32), :]
            zs[side, x] = column.astype(BF16)
            for ys, y in ((0, 0), (1, 15)):
                yz[side, ys, x : x + 1, :] = column[y : y + 1]

    pl.semaphore_wait(barrier, greeted)

    def halo(shift):
        dg, da, db = shift
        x = {-1: 0, 1: 1}.get(dg)
        px = {-1: 3, 1: 0}.get(dg)
        y = {-1: 0, 1: 15}.get(da)
        py = {-1: 17, 1: 0}.get(da)
        s = {-1: 0, 1: 1}.get(db)
        if db == 0:
            if da == 0:
                src, dst = pad.at[x + 1, 1:17], pad.at[px, 1:17]
            elif dg == 0:
                src, dst = pad.at[1:3, y + 1], pad.at[1:3, py]
            else:
                src, dst = pad.at[x + 1, y + 1], pad.at[px, py]
        elif da == 0:
            if dg == 0:
                src, dst = zs.at[s], zh.at[1 - s, 1:3]
            else:
                src, dst = zs.at[s, x], zh.at[1 - s, px]
        else:
            ys = {-1: 0, 1: 1}[da]
            src, dst = yz.at[s, ys], ch.at[1 - s, 1 - ys, {-1: 2, 0: 1, 1: 0}[dg]]
        number = SHIFTS.index(shift)
        return pltpu.make_async_remote_copy(
            src_ref=src, dst_ref=dst, send_sem=halo_send.at[number], recv_sem=halo_recv.at[number],
            device_id=device(*shift), device_id_type=MESH,
        )

    def halo_sent():
        for shift in SHIFTS:
            @pl.when(there(*shift))
            def _():
                halo(shift).wait_send()

    def halo_wait(shifts):
        for shift in shifts:
            @pl.when(there(*(-i for i in shift)))
            def _():
                halo(shift).wait_recv()

    for shift in ring:
        @pl.when(there(*shift))
        def _():
            halo(shift).start()

    def shard_rows(first, which):
        return w5b.at[pl.ds(pl.multiple_of(first + 48 * which, 16), 48), :]

    def shard_copy():
        return pltpu.make_async_remote_copy(
            src_ref=shard_rows(0, core), dst_ref=shard_rows(96, core), send_sem=shard_send.at[0], recv_sem=shard_recv.at[0],
            device_id={"gy": other}, device_id_type=MESH,
        )

    def shard_relay():
        return pltpu.make_async_remote_copy(
            src_ref=shard_rows(96, core), dst_ref=shard_rows(96, core), send_sem=shard_send.at[1], recv_sem=shard_recv.at[1],
            device_id={"gx": g + 1 - 2 * core}, device_id_type=MESH,
        )

    for load in w5_loads:
        load.wait()
    shard_copy().start()

    def widen(x):
        for y in range(18):
            if not (x in (1, 2) and 1 <= y <= 16):
                row = (x * 18 + y) * 32 + 8
                wide[row : row + 16, :] = pad[x, y].astype(F32)
        for side, at in ((0, 7), (1, 24)):
            wide[pl.ds((x * 18 + 1) * 32 + at, 16, stride=32), :] = zh[side, x].astype(F32)
            for ys, y in ((0, 0), (1, 17)):
                source, row = ((0, 1), (1, 0), (1, 1), (2, 0))[x]
                first = (x * 18 + y) * 32 + at
                wide[first : first + 1, :] = ch[side, ys, source, row : row + 1, :]
        for y in range(18):
            row = (x * 18 + y) * 32
            left = wide[row + 7 : row + 23, :].astype(BF16)
            right = wide[row + 9 : row + 25, :].astype(BF16)
            taps[x, y * 16 : y * 16 + 16, :] = jnp.concatenate([left, pad[x, y], right], axis=-1)

    def around(x):
        return jnp.concatenate([taps[x, dy * 16 : dy * 16 + 256, :] for dy in range(3)], axis=-1)

    halo_wait([shift for shift in SHIFTS if shift[0] == 0])
    for x in (1, 2):
        widen(x)
    w4_load.wait()
    span = 9 * CIN
    own = jnp.concatenate([around(1), around(2)], axis=-1)
    for x in (0, 1):
        first = (1 - x) * span
        hidden[x] = jnp.dot(own, w4b[first : first + 2 * span, :], preferred_element_type=F32)
    halo_wait([shift for shift in SHIFTS if shift[0]])
    for x in (0, 3):
        widen(x)
    tops = jnp.maximum(
        hidden[0] + jnp.dot(around(0), w4b[:span, :], preferred_element_type=F32),
        hidden[1] + jnp.dot(around(3), w4b[2 * span :, :], preferred_element_type=F32),
    )
    tops = jnp.max(tops.reshape(8, 2, 16, C4), axis=1).reshape(128, C4)
    for lanes in range(2):
        pool[lanes] = tops[:, lanes * 128 : lanes * 128 + 128]
    for lanes in range(2):
        tops = jnp.maximum(pool[lanes, pl.ds(0, 64, stride=2), :], pool[lanes, pl.ds(1, 64, stride=2), :])
        block[:, lanes * 128 : lanes * 128 + 128] = jnp.where(tops > 0, tops, 0.3 * tops).astype(BF16)

    mine = (a - 2 * half) * ngz + b
    offsets = [(di, db) for di in range(2) for db in range(ngz) if (di, db) != (0, 0)]

    def spread(di, db):
        number = di * ngz + db
        return pltpu.make_async_remote_copy(
            src_ref=block, dst_ref=blocks.at[mine], send_sem=block_send.at[number], recv_sem=block_recv.at[number],
            device_id={"gy": beside if di else a, "gz": lax.rem(b + db, ngz)}, device_id_type=MESH,
        )

    def rim_copy(t, db):
        return pltpu.make_async_remote_copy(
            src_ref=rim, dst_ref=rims.at[b], send_sem=rim_send.at[t, db], recv_sem=rim_recv.at[db],
            device_id={"gy": 2 * (1 - half) + t, "gz": lax.rem(b + db, ngz)}, device_id_type=MESH,
        )

    for at, first in ((1, 56), (2, 0)):
        @pl.when(a == at)
        def _():
            rim[...] = block[first : first + 8, :].astype(F32)

    for di, db in offsets:
        spread(di, db).start()

    @pl.when(jnp.logical_or(a == 1, a == 2))
    def _():
        for t in range(2):
            for db in range(ngz):
                rim_copy(t, db).start()

    blocks[mine] = block[...]
    halo_sent()
    shard_copy().wait_recv()
    shard_relay().start()

    def spread_sent():
        shard_copy().wait_send()
        shard_relay().wait_send()
        for di, db in offsets:
            spread(di, db).wait_send()

        @pl.when(jnp.logical_or(a == 1, a == 2))
        def _():
            for t in range(2):
                for db in range(ngz):
                    rim_copy(t, db).wait_send()

    def lay(first, rows):
        for dz in range(3):
            for row in range(rows):
                slab[dz, first + row] = broad[first + row, 7 + dz : 39 + dz, :].astype(BF16)

    for di, row in ((0, a - 2 * half), (1, 1 - a + 2 * half)):
        for db in range(ngz):
            if (di, db) != (0, 0):
                spread(di, db).wait_recv()
        for z in range(ngz):
            broad[pl.ds(1 + 8 * row, 8), 8 + 8 * z : 16 + 8 * z, :] = blocks[row * ngz + z].astype(F32).reshape(8, 8, C4)
        lay(1 + 8 * row, 8)
    for db in range(ngz):
        rim_copy(0, db).wait_recv()
    for z in range(ngz):
        broad[17 * (1 - half), 8 + 8 * z : 16 + 8 * z, :] = rims[z]
    lay(17 * (1 - half), 1)
    shard_relay().wait_recv()

    parts = [(p, k) for p in (1, 0) for k in (0, 2, 1) if (p, k) != (0, 1)]

    def part_when(k, sender):
        if k == 1:
            return lambda f: f()
        if (k == 0) == sender:
            return pl.when(g < ngx - 1)
        return pl.when(g > 0)

    def part_copy(p, k, q):
        return pltpu.make_async_remote_copy(
            src_ref=sent.at[p, k, q], dst_ref=got.at[p, k, q], send_sem=part_send.at[p, k, q], recv_sem=part_recv.at[p, k, q],
            device_id={"gx": g + 1 - k, "gy": other if p else a}, device_id_type=MESH,
        )

    lane = lax.broadcasted_iota(jnp.int32, (64, 128), 1)

    def group(rows, j):
        tile, k = divmod(j, 4)
        moved = [
            pltpu.roll(rows[64 * u : 64 * u + 64, 128 * tile : 128 * tile + 128], (32 * (u - k)) % 128, axis=1)
            if u != k else rows[64 * u : 64 * u + 64, 128 * tile : 128 * tile + 128]
            for u in range(4)
        ]
        return jnp.where(lane < 64, jnp.where(lane < 32, moved[0], moved[1]), jnp.where(lane < 96, moved[2], moved[3]))

    totals = []
    for q in range(2):
        lhs = jnp.concatenate(
            [slab[dz, 8 * q + dy : 8 * q + dy + 8].reshape(256, C4) for dz in range(3) for dy in range(3)], axis=-1
        )
        totals.append(lax.dot_general(lhs, w5b[...], (((1,), (1,)), ((), ())), preferred_element_type=F32))
    for p, k in parts:
        for q in range(2):
            sent[p, k, q] = group(totals[q], 3 * p + k).astype(BF16)

        @part_when(k, True)
        def _():
            for q in range(2):
                part_copy(p, k, q).start()

    for q in range(2):
        packed[0, q] = group(totals[q], 1)

    spread_sent()
    for q in range(2):
        part_copy(1, 1, q).wait_recv()
        packed[1, q] = got[1, 1, q].astype(F32)
    for k in (0, 2):
        @part_when(k, False)
        def _():
            for p in range(2):
                for q in range(2):
                    part_copy(p, k, q).wait_recv()
                    packed[p, q] += got[p, k, q].astype(F32)

    out[half] = packed[0].astype(BF16)
    out[1 - half] = packed[1].astype(BF16)

    finish(9)


def body(sizes, volume, conv4_weight, conv5_weight):
    ngx, ngy, ngz = sizes
    any_space = pl.BlockSpec(memory_space=pl.ANY)
    packed = pl.pallas_call(
        functools.partial(kernel, sizes),
        out_shape=jax.ShapeDtypeStruct((2, 2, 64, 128), BF16),
        in_specs=[any_space] * 3,
        out_specs=pl.BlockSpec(memory_space=pltpu.VMEM),
        scratch_shapes=[
            pltpu.VMEM((4, 18, 16, CIN), BF16),
            pltpu.VMEM((4 * 18 * 32, CIN), F32),
            pltpu.VMEM((4, 18 * 16, 3 * CIN), BF16),
            pltpu.VMEM((27 * CIN, C4), BF16),
            pltpu.VMEM((256, 9 * C4), BF16),
            pltpu.VMEM((2, 2, 16, CIN), BF16),
            pltpu.VMEM((2, 2, 8, CIN), F32),
            pltpu.VMEM((2, 4, 16, CIN), BF16),
            pltpu.VMEM((2, 2, 3, 8, CIN), F32),
            pltpu.VMEM((2, 256, C4), F32),
            pltpu.VMEM((2, 128, 128), F32),
            pltpu.VMEM((64, C4), BF16),
            pltpu.VMEM((2 * ngz, 64, C4), BF16),
            pltpu.VMEM((8, C4), F32),
            pltpu.VMEM((ngz, 8, C4), F32),
            pltpu.VMEM((3, 18, PLANE, C4), BF16),
            pltpu.VMEM((18, 48, C4), F32),
            pltpu.VMEM((2, 3, 2, 64, 128), BF16),
            pltpu.VMEM((2, 3, 2, 64, 128), BF16),
            pltpu.VMEM((2, 2, 64, 128), F32),
            pltpu.SemaphoreType.DMA((29,)),
            pltpu.SemaphoreType.DMA((26,)),
            pltpu.SemaphoreType.DMA((26,)),
            pltpu.SemaphoreType.DMA((2 * ngz,)),
            pltpu.SemaphoreType.DMA((2 * ngz,)),
            pltpu.SemaphoreType.DMA((2, ngz)),
            pltpu.SemaphoreType.DMA((ngz,)),
            pltpu.SemaphoreType.DMA((2, 3, 2)),
            pltpu.SemaphoreType.DMA((2, 3, 2)),
            pltpu.SemaphoreType.DMA((2,)),
            pltpu.SemaphoreType.DMA((2,)),
        ],
        compiler_params=pltpu.CompilerParams(
            collective_id=0, has_side_effects=True, vmem_limit_bytes=40 * 1024 * 1024
        ),
    )(
        *(pltpu.with_memory_space_constraint(x, pltpu.HBM) for x in (volume, conv4_weight.reshape(27 * CIN, C4), jnp.swapaxes(conv5_weight, 3, 4))),
    )
    cells = packed.reshape(4, 2, PLANE, 4, FILTERS).transpose(0, 3, 1, 2, 4)
    return cells.reshape(1, PLANE, PLANE, FILTERS)


def solution(mesh):
    sizes = (mesh.shape["gx"], mesh.shape["gy"], mesh.shape["gz"])
    return jax.shard_map(
        functools.partial(body, sizes),
        mesh=mesh,
        in_specs=(
            P(("sample", "gx"), "gy", "gz", None),
            P(),
            P(None, None, None, None, ("gy", "gz")),
        ),
        out_specs=P(("sample", "gx"), None, None, ("gy", "gz")),
        check_vma=False,
    )
```

```python
import functools

import jax
import jax.numpy as jnp
from jax import lax
from jax.experimental import pallas as pl
from jax.experimental.pallas import tpu as pltpu
from jax.sharding import PartitionSpec as P

MESH = pl.DeviceIdType.MESH
BF16, F32 = jnp.bfloat16, jnp.float32
CIN, C4, FILTERS = 128, 256, 32
PLANE = 32
SHIFTS = [(i, j, k) for i in (-1, 0, 1) for j in (-1, 0, 1) for k in (-1, 0, 1) if (i, j, k) != (0, 0, 0)]


def kernel(
    sizes, v, w4, w5, out,
    pad, wide, taps, w4b, w5b, zs, yz, zh, ch, hidden, early, late, pool, block, blocks, rim, rims, slab, broad, sent, got, packed,
    load_sem, halo_send, halo_recv, block_send, block_recv, rim_send, rim_recv, part_send, part_recv, shard_send, shard_recv,
):
    ngx, ngy, ngz = sizes
    g, a, b = lax.axis_index("gx"), lax.axis_index("gy"), lax.axis_index("gz")
    half = lax.div(a, 2)
    core = lax.rem(g, 2)
    other = ngy - 1 - a
    beside = 4 * half + 1 - a

    def there(dg, da, db):
        ok = None
        for at, step, n in ((g, dg, ngx), (a, da, ngy), (b, db, ngz)):
            if step:
                fine = (at > 0) if step < 0 else (at < n - 1)
                ok = fine if ok is None else jnp.logical_and(ok, fine)
        return ok

    def device(dg, da, db):
        return {"gx": g + dg, "gy": a + da, "gz": b + db}

    own_load = pltpu.make_async_copy(v, pad.at[1:3, 1:17], load_sem.at[0])
    own_load.start()
    w4_load = pltpu.make_async_copy(w4, w4b, load_sem.at[1])
    w4_load.start()
    w5_loads = [
        pltpu.make_async_copy(w5.at[dx], w5b.at[:, dx * FILTERS : (dx + 1) * FILTERS, :], load_sem.at[2 + dx]) for dx in range(3)
    ]
    for load in w5_loads:
        load.start()

    barrier = pltpu.get_barrier_semaphore()
    near_a = {da: lax.rem(a + da + ngy, ngy) for da in (-1, 0, 1)}
    near_b = {db: lax.rem(b + db + ngz, ngz) for db in (-1, 0, 1)}

    def greet(dg):
        for da, db in sorted(((i, j) for i in (-1, 0, 1) for j in (-1, 0, 1)), key=lambda at: -abs(at[0]) - abs(at[1])):
            if (dg, da, db) != (0, 0, 0):
                pl.semaphore_signal(
                    barrier, inc=1, device_id={"gx": g + dg, "gy": near_a[da], "gz": near_b[db]}, device_id_type=MESH
                )

    pl.when(g < ngx - 1)(lambda: greet(1))
    pl.when(g > 0)(lambda: greet(-1))
    greet(0)
    sides = (g > 0).astype(jnp.int32) + (g < ngx - 1).astype(jnp.int32)
    greeted = 9 * sides + 8

    def finish(stage):
        if stage < 2:
            w4_load.wait()
        if stage < 2:
            for load in w5_loads:
                load.wait()
        if stage == 2:
            halo_wait([shift for shift in SHIFTS if shift[0]])
            w4_load.wait()
        if 2 <= stage < 4:
            halo_sent()
            for piece in range(3):
                shard_copy(piece).wait_send()
                shard_copy(piece).wait_recv()
        if stage == 4:
            spread_sent()
        if stage >= 5:
            for p, k in parts:
                @part_when(k, True)
                def _():
                    for q in range(2):
                        part_copy(p, k, q).wait_send()

    yz[...] = jnp.zeros(yz.shape, F32)
    own_load.wait()
    for x in (1, 2):
        for y in range(1, 17):
            row = (x * 18 + y) * 32 + 8
            wide[row : row + 16, :] = pad[x, y].astype(F32)
    for side, z in ((0, 0), (1, 15)):
        for x in (0, 1):
            first = ((x + 1) * 18 + 1) * 32 + 8 + z
            column = wide[pl.ds(first, 16, stride=32), :]
            zs[side, x] = column.astype(BF16)
            for ys, y in ((0, 0), (1, 15)):
                yz[side, ys, x : x + 1, :] = column[y : y + 1]

    pl.semaphore_wait(barrier, greeted)

    def halo(shift):
        dg, da, db = shift
        x = {-1: 0, 1: 1}.get(dg)
        px = {-1: 3, 1: 0}.get(dg)
        y = {-1: 0, 1: 15}.get(da)
        py = {-1: 17, 1: 0}.get(da)
        s = {-1: 0, 1: 1}.get(db)
        if db == 0:
            if da == 0:
                src, dst = pad.at[x + 1, 1:17], pad.at[px, 1:17]
            elif dg == 0:
                src, dst = pad.at[1:3, y + 1], pad.at[1:3, py]
            else:
                src, dst = pad.at[x + 1, y + 1], pad.at[px, py]
        elif da == 0:
            if dg == 0:
                src, dst = zs.at[s], zh.at[1 - s, 1:3]
            else:
                src, dst = zs.at[s, x], zh.at[1 - s, px]
        else:
            ys = {-1: 0, 1: 1}[da]
            src, dst = yz.at[s, ys], ch.at[1 - s, 1 - ys, {-1: 2, 0: 1, 1: 0}[dg]]
        number = SHIFTS.index(shift)
        return pltpu.make_async_remote_copy(
            src_ref=src, dst_ref=dst, send_sem=halo_send.at[number], recv_sem=halo_recv.at[number],
            device_id=device(*shift), device_id_type=MESH,
        )

    def halo_sent():
        for shift in SHIFTS:
            @pl.when(there(*shift))
            def _():
                halo(shift).wait_send()

    def halo_wait(shifts):
        for shift in shifts:
            @pl.when(there(*(-i for i in shift)))
            def _():
                halo(shift).wait_recv()

    for shift in sorted(SHIFTS, key=lambda shift: (shift[0] != 0, -sum(map(abs, shift)))):
        @pl.when(there(*shift))
        def _():
            halo(shift).start()
    @pl.when(g == 0)
    def _():
        pad[0] = jnp.zeros(pad.shape[1:], BF16)
        zh[:, 0] = jnp.zeros((2, 16, CIN), BF16)
        ch[:, :, 0] = jnp.zeros((2, 2, 8, CIN), F32)

    @pl.when(g == ngx - 1)
    def _():
        pad[3] = jnp.zeros(pad.shape[1:], BF16)
        zh[:, 3] = jnp.zeros((2, 16, CIN), BF16)
        ch[:, :, 2] = jnp.zeros((2, 2, 8, CIN), F32)

    for side, edge_at in ((0, 0), (1, ngy - 1)):
        @pl.when(a == edge_at)
        def _():
            pad[:, 17 * side] = jnp.zeros((4, 16, CIN), BF16)
            ch[:, side] = jnp.zeros((2, 3, 8, CIN), F32)

    for side, edge_at in ((0, 0), (1, ngz - 1)):
        @pl.when(b == edge_at)
        def _():
            zh[side] = jnp.zeros((4, 16, CIN), BF16)
            ch[side] = jnp.zeros((2, 3, 8, CIN), F32)

    for dz in range(3):
        slab[dz, 17 * half] = jnp.zeros((PLANE, C4), BF16)
    broad[:, 0:8] = jnp.zeros((18, 8, C4), F32)
    broad[:, 40:48] = jnp.zeros((18, 8, C4), F32)


    def shard_rows(first, piece):
        return w5b.at[3 * piece : 3 * piece + 3, pl.ds(pl.multiple_of(first + 48 * core, 16), 48), :]

    def shard_copy(piece):
        return pltpu.make_async_remote_copy(
            src_ref=shard_rows(0, piece), dst_ref=shard_rows(96, piece),
            send_sem=shard_send.at[0, piece], recv_sem=shard_recv.at[0, piece],
            device_id={"gy": other}, device_id_type=MESH,
        )

    def shard_relay(piece):
        return pltpu.make_async_remote_copy(
            src_ref=shard_rows(96, piece), dst_ref=shard_rows(96, piece),
            send_sem=shard_send.at[1, piece], recv_sem=shard_recv.at[1, piece],
            device_id={"gx": g + 1 - 2 * core}, device_id_type=MESH,
        )

    for load in w5_loads:
        load.wait()
    for piece in range(3):
        shard_copy(piece).start()

    def widen(x):
        for y in range(18):
            if not (x in (1, 2) and 1 <= y <= 16):
                row = (x * 18 + y) * 32 + 8
                wide[row : row + 16, :] = pad[x, y].astype(F32)
        for side, at in ((0, 7), (1, 24)):
            wide[pl.ds((x * 18 + 1) * 32 + at, 16, stride=32), :] = zh[side, x].astype(F32)
            for ys, y in ((0, 0), (1, 17)):
                source, row = ((0, 1), (1, 0), (1, 1), (2, 0))[x]
                first = (x * 18 + y) * 32 + at
                wide[first : first + 1, :] = ch[side, ys, source, row : row + 1, :]
        for y in range(18):
            row = (x * 18 + y) * 32
            left = wide[row + 7 : row + 23, :].astype(BF16)
            right = wide[row + 9 : row + 25, :].astype(BF16)
            taps[x, y * 16 : y * 16 + 16, :] = jnp.concatenate([left, pad[x, y], right], axis=-1)

    def around(x):
        return jnp.concatenate([taps[x, dy * 16 : dy * 16 + 256, :] for dy in range(3)], axis=-1)

    halo_wait([shift for shift in SHIFTS if shift[0] == 0])
    for x in (1, 2):
        widen(x)
    w4_load.wait()
    span = 9 * CIN
    own = jnp.concatenate([around(1), around(2)], axis=-1)
    for x in (0, 1):
        first = (1 - x) * span
        hidden[x] = jnp.dot(own, w4b[first : first + 2 * span, :], preferred_element_type=F32)
    halo_wait([shift for shift in SHIFTS if shift[0]])
    for x in (0, 3):
        widen(x)
    tops = jnp.maximum(
        hidden[0] + jnp.dot(around(0), w4b[:span, :], preferred_element_type=F32),
        hidden[1] + jnp.dot(around(3), w4b[2 * span :, :], preferred_element_type=F32),
    )
    tops = jnp.max(tops.reshape(8, 2, 16, C4), axis=1).reshape(128, C4)
    for lanes in range(2):
        pool[lanes] = tops[:, lanes * 128 : lanes * 128 + 128]
    for lanes in range(2):
        tops = jnp.maximum(pool[lanes, pl.ds(0, 64, stride=2), :], pool[lanes, pl.ds(1, 64, stride=2), :])
        block[:, lanes * 128 : lanes * 128 + 128] = jnp.where(tops > 0, tops, 0.3 * tops).astype(BF16)

    mine = (a - 2 * half) * ngz + b
    offsets = [(di, db) for di in range(2) for db in range(ngz) if (di, db) != (0, 0)]

    def spread(di, db):
        number = di * ngz + db
        return pltpu.make_async_remote_copy(
            src_ref=block, dst_ref=blocks.at[mine], send_sem=block_send.at[number], recv_sem=block_recv.at[number],
            device_id={"gy": beside if di else a, "gz": lax.rem(b + db, ngz)}, device_id_type=MESH,
        )

    def rim_copy(t, db):
        return pltpu.make_async_remote_copy(
            src_ref=rim, dst_ref=rims.at[b], send_sem=rim_send.at[t, db], recv_sem=rim_recv.at[db],
            device_id={"gy": 2 * (1 - half) + t, "gz": lax.rem(b + db, ngz)}, device_id_type=MESH,
        )

    for at, first in ((1, 56), (2, 0)):
        @pl.when(a == at)
        def _():
            rim[...] = block[first : first + 8, :]

    @pl.when(jnp.logical_or(a == 1, a == 2))
    def _():
        for db in (2, 1, 3, 0):
            for t in range(2):
                rim_copy(t, db).start()

    for di, db in ((1, 2), (0, 2), (1, 1), (1, 3), (0, 1), (0, 3), (1, 0)):
        spread(di, db).start()

    blocks[mine] = block[...]
    halo_sent()
    for piece in range(3):
        shard_copy(piece).wait_recv()
        shard_relay(piece).start()

    def spread_sent():
        for piece in range(3):
            shard_copy(piece).wait_send()
            shard_relay(piece).wait_send()
        for di, db in offsets:
            spread(di, db).wait_send()

        @pl.when(jnp.logical_or(a == 1, a == 2))
        def _():
            for t in range(2):
                for db in range(ngz):
                    rim_copy(t, db).wait_send()

    def lay(first, rows):
        for dz in range(3):
            for row in range(rows):
                slab[dz, first + row] = broad[first + row, 7 + dz : 39 + dz, :].astype(BF16)

    at = a - 2 * half
    taps_w5 = (((1,), (1,)), ((), ()))

    def settle(di, row):
        for db in range(ngz):
            if (di, db) != (0, 0):
                spread(di, db).wait_recv()
        for z in range(ngz):
            broad[pl.ds(1 + 8 * row, 8), 8 + 8 * z : 16 + 8 * z, :] = blocks[row * ngz + z].astype(F32).reshape(8, 8, C4)
        lay(1 + 8 * row, 8)

    def all_taps(numbers):
        return jnp.concatenate([w5b[number] for number in numbers], axis=-1)

    def rows_of(first, rows):
        return jnp.concatenate(
            [slab[dz, pl.ds(first + dy, rows)].reshape(rows * PLANE, C4) for dy in range(3) for dz in range(3)], axis=-1
        )

    settle(0, at)
    for dz in range(3):
        for row in (8 * at, 8 * at + 9):
            slab[dz, row] = jnp.zeros((PLANE, C4), BF16)
    for piece in range(3):
        shard_relay(piece).wait_recv()
    for part in range(2):
        early[128 * part : 128 * part + 128, :192] = lax.dot_general(
            rows_of(8 * at + 4 * part, 4), all_taps(range(9)), taps_w5, preferred_element_type=F32
        )
    settle(1, 1 - at)
    for db in range(ngz):
        rim_copy(0, db).wait_recv()
    for z in range(ngz):
        broad[17 * (1 - half), 8 + 8 * z : 16 + 8 * z, :] = rims[z].astype(F32)
    lay(17 * (1 - half), 1)

    parts = [(p, k) for p in (1, 0) for k in (0, 2, 1) if (p, k) != (0, 1)]

    def part_when(k, sender):
        if k == 1:
            return lambda f: f()
        if (k == 0) == sender:
            return pl.when(g < ngx - 1)
        return pl.when(g > 0)

    def part_copy(p, k, q):
        return pltpu.make_async_remote_copy(
            src_ref=sent.at[p, k, q], dst_ref=got.at[p, k, q], send_sem=part_send.at[p, k, q], recv_sem=part_recv.at[p, k, q],
            device_id={"gx": g + 1 - k, "gy": other if p else a}, device_id_type=MESH,
        )

    lane = lax.broadcasted_iota(jnp.int32, (64, 128), 1)

    def group(rows, j):
        tile, k = divmod(j, 4)
        moved = [
            pltpu.roll(rows[64 * u : 64 * u + 64, 128 * tile : 128 * tile + 128], (32 * (u - k)) % 128, axis=1)
            if u != k else rows[64 * u : 64 * u + 64, 128 * tile : 128 * tile + 128]
            for u in range(4)
        ]
        return jnp.where(lane < 64, jnp.where(lane < 32, moved[0], moved[1]), jnp.where(lane < 96, moved[2], moved[3]))

    def send_parts(total, slot):
        for p, k in parts:
            sent[p, k, slot] = group(total, 3 * p + k).astype(BF16)

            @part_when(k, True)
            def _():
                part_copy(p, k, slot).start()

        packed[0, slot] = group(total, 1)

    for row, first, dy in ((8 * at, 0, 0), (8 * at + 9, 224, 2)):
        early[first : first + PLANE, :192] += lax.dot_general(
            jnp.concatenate([slab[dz, row] for dz in range(3)], axis=-1),
            all_taps(range(3 * dy, 3 * dy + 3)),
            taps_w5, preferred_element_type=F32,
        )
    send_parts(early[...], 0)
    for part in range(2):
        late[128 * part : 128 * part + 128, :192] = lax.dot_general(
            rows_of(8 * (1 - at) + 4 * part, 4), all_taps(range(9)), taps_w5, preferred_element_type=F32
        )
    send_parts(late[...], 1)

    spread_sent()
    for slot in range(2):
        part_copy(1, 1, slot).wait_recv()
        packed[1, slot] = got[1, 1, slot].astype(F32)
    for k in (0, 2):
        @part_when(k, False)
        def _():
            for p in range(2):
                for slot in range(2):
                    part_copy(p, k, slot).wait_recv()
                    packed[p, slot] += got[p, k, slot].astype(F32)

    for p, place in ((0, half), (1, 1 - half)):
        for slot in range(2):
            out[place, at if p == slot else 1 - at] = packed[p, slot].astype(BF16)

    finish(9)


def body(sizes, volume, conv4_weight, conv5_weight):
    ngx, ngy, ngz = sizes
    any_space = pl.BlockSpec(memory_space=pl.ANY)
    packed = pl.pallas_call(
        functools.partial(kernel, sizes),
        out_shape=jax.ShapeDtypeStruct((2, 2, 64, 128), BF16),
        in_specs=[any_space] * 3,
        out_specs=pl.BlockSpec(memory_space=pltpu.VMEM),
        scratch_shapes=[
            pltpu.VMEM((4, 18, 16, CIN), BF16),
            pltpu.VMEM((4 * 18 * 32, CIN), F32),
            pltpu.VMEM((4, 18 * 16, 3 * CIN), BF16),
            pltpu.VMEM((27 * CIN, C4), BF16),
            pltpu.VMEM((9, 192, C4), BF16),
            pltpu.VMEM((2, 2, 16, CIN), BF16),
            pltpu.VMEM((2, 2, 8, CIN), F32),
            pltpu.VMEM((2, 4, 16, CIN), BF16),
            pltpu.VMEM((2, 2, 3, 8, CIN), F32),
            pltpu.VMEM((2, 256, C4), F32),
            pltpu.VMEM((256, 256), F32),
            pltpu.VMEM((256, 256), F32),
            pltpu.VMEM((2, 128, 128), F32),
            pltpu.VMEM((64, C4), BF16),
            pltpu.VMEM((2 * ngz, 64, C4), BF16),
            pltpu.VMEM((8, C4), BF16),
            pltpu.VMEM((ngz, 8, C4), BF16),
            pltpu.VMEM((3, 18, PLANE, C4), BF16),
            pltpu.VMEM((18, 48, C4), F32),
            pltpu.VMEM((2, 3, 2, 64, 128), BF16),
            pltpu.VMEM((2, 3, 2, 64, 128), BF16),
            pltpu.VMEM((2, 2, 64, 128), F32),
            pltpu.SemaphoreType.DMA((5,)),
            pltpu.SemaphoreType.DMA((26,)),
            pltpu.SemaphoreType.DMA((26,)),
            pltpu.SemaphoreType.DMA((2 * ngz,)),
            pltpu.SemaphoreType.DMA((2 * ngz,)),
            pltpu.SemaphoreType.DMA((2, ngz)),
            pltpu.SemaphoreType.DMA((ngz,)),
            pltpu.SemaphoreType.DMA((2, 3, 2)),
            pltpu.SemaphoreType.DMA((2, 3, 2)),
            pltpu.SemaphoreType.DMA((2, 3)),
            pltpu.SemaphoreType.DMA((2, 3)),
        ],
        compiler_params=pltpu.CompilerParams(
            collective_id=0, has_side_effects=True, vmem_limit_bytes=40 * 1024 * 1024
        ),
    )(
        *(pltpu.with_memory_space_constraint(x, pltpu.HBM) for x in (volume, conv4_weight.reshape(27 * CIN, C4), jnp.swapaxes(conv5_weight, 3, 4).reshape(3, 9, FILTERS, C4))),
    )
    cells = packed.reshape(4, 2, PLANE, 4, FILTERS).transpose(0, 3, 1, 2, 4)
    return cells.reshape(1, PLANE, PLANE, FILTERS)


def solution(mesh):
    sizes = (mesh.shape["gx"], mesh.shape["gy"], mesh.shape["gz"])
    return jax.shard_map(
        functools.partial(body, sizes),
        mesh=mesh,
        in_specs=(
            P(("sample", "gx"), "gy", "gz", None),
            P(),
            P(None, None, None, None, ("gy", "gz")),
        ),
        out_specs=P(("sample", "gx"), None, None, ("gy", "gz")),
        check_vma=False,
    )
```

```python
import functools

import jax
import jax.numpy as jnp
from jax import lax
from jax.experimental import pallas as pl
from jax.experimental.pallas import tpu as pltpu
from jax.sharding import PartitionSpec as P

MESH = pl.DeviceIdType.MESH
BF16, F32 = jnp.bfloat16, jnp.float32
CIN, C4, FILTERS = 128, 256, 32
PLANE = 32
SHIFTS = [(i, j, k) for i in (-1, 0, 1) for j in (-1, 0, 1) for k in (-1, 0, 1) if (i, j, k) != (0, 0, 0)]


def kernel(
    sizes, v, w4, w5, out,
    pad, wide, taps, w4b, w5b, zs, yz, zh, ch, hidden, early, late, pool, block, blocks, rim, rims, slab, broad, sent, got, packed,
    known, load_sem, halo_send, halo_recv, block_send, block_recv, rim_send, rim_recv, part_send, part_recv, shard_send, shard_recv,
):
    ngx, ngy, ngz = sizes
    g, a, b = lax.axis_index("gx"), lax.axis_index("gy"), lax.axis_index("gz")
    half = lax.div(a, 2)
    core = lax.rem(g, 2)
    other = ngy - 1 - a
    beside = 4 * half + 1 - a

    def there(dg, da, db):
        ok = None
        for at, step, n in ((g, dg, ngx), (a, da, ngy), (b, db, ngz)):
            if step:
                fine = (at > 0) if step < 0 else (at < n - 1)
                ok = fine if ok is None else jnp.logical_and(ok, fine)
        return ok

    def device(dg, da, db):
        return {"gx": g + dg, "gy": a + da, "gz": b + db}

    own_load = pltpu.make_async_copy(v, pad.at[1:3, 1:17], load_sem.at[0])
    own_load.start()
    w4_load = pltpu.make_async_copy(w4, w4b, load_sem.at[1])
    w4_load.start()
    w5_loads = [
        pltpu.make_async_copy(w5.at[dx], w5b.at[:, dx * FILTERS : (dx + 1) * FILTERS, :], load_sem.at[2 + dx]) for dx in range(3)
    ]
    for load in w5_loads:
        load.start()

    barrier = pltpu.get_barrier_semaphore()
    for shift in sorted(SHIFTS, key=lambda shift: -sum(map(abs, shift))):
        @pl.when(there(*shift))
        def _():
            pl.semaphore_signal(barrier, inc=1, device_id=device(*shift), device_id_type=MESH)
    pl.semaphore_signal(barrier, inc=1, device_id={"gy": other}, device_id_type=MESH)

    def near(position, n):
        return 1 + (position > 0).astype(jnp.int32) + (position < n - 1).astype(jnp.int32)

    greeted = near(g, ngx) * near(a, ngy) * near(b, ngz)

    def finish(stage):
        if stage < 2:
            w4_load.wait()
        if stage < 2:
            for load in w5_loads:
                load.wait()
        if stage == 2:
            halo_wait([shift for shift in SHIFTS if shift[0]])
            w4_load.wait()
        if 2 <= stage < 4:
            halo_sent()
            for piece in range(3):
                shard_copy(piece).wait_send()
                shard_copy(piece).wait_recv()
        if stage == 4:
            spread_sent()
        if stage >= 5:
            for p, k in parts:
                @part_when(k, True)
                def _():
                    for q in range(2):
                        part_copy(p, k, q).wait_send()

    yz[...] = jnp.zeros(yz.shape, F32)
    own_load.wait()
    for x in (1, 2):
        for y in range(1, 17):
            row = (x * 18 + y) * 32 + 8
            wide[row : row + 16, :] = pad[x, y].astype(F32)
    for side, z in ((0, 0), (1, 15)):
        for x in (0, 1):
            first = ((x + 1) * 18 + 1) * 32 + 8 + z
            column = wide[pl.ds(first, 16, stride=32), :]
            zs[side, x] = column.astype(BF16)
            for ys, y in ((0, 0), (1, 15)):
                yz[side, ys, x : x + 1, :] = column[y : y + 1]

    pl.semaphore_wait(barrier, greeted)

    def halo(shift):
        dg, da, db = shift
        x = {-1: 0, 1: 1}.get(dg)
        px = {-1: 3, 1: 0}.get(dg)
        y = {-1: 0, 1: 15}.get(da)
        py = {-1: 17, 1: 0}.get(da)
        s = {-1: 0, 1: 1}.get(db)
        if db == 0:
            if da == 0:
                src, dst = pad.at[x + 1, 1:17], pad.at[px, 1:17]
            elif dg == 0:
                src, dst = pad.at[1:3, y + 1], pad.at[1:3, py]
            else:
                src, dst = pad.at[x + 1, y + 1], pad.at[px, py]
        elif da == 0:
            if dg == 0:
                src, dst = zs.at[s], zh.at[1 - s, 1:3]
            else:
                src, dst = zs.at[s, x], zh.at[1 - s, px]
        else:
            ys = {-1: 0, 1: 1}[da]
            src, dst = yz.at[s, ys], ch.at[1 - s, 1 - ys, {-1: 2, 0: 1, 1: 0}[dg]]
        number = SHIFTS.index(shift)
        return pltpu.make_async_remote_copy(
            src_ref=src, dst_ref=dst, send_sem=halo_send.at[number], recv_sem=halo_recv.at[number],
            device_id=device(*shift), device_id_type=MESH,
        )

    def halo_sent():
        for shift in SHIFTS:
            @pl.when(there(*shift))
            def _():
                halo(shift).wait_send()

    def halo_wait(shifts):
        for shift in shifts:
            @pl.when(there(*(-i for i in shift)))
            def _():
                halo(shift).wait_recv()

    for shift in sorted(SHIFTS, key=lambda shift: (shift[0] != 0, -sum(map(abs, shift)))):
        @pl.when(there(*shift))
        def _():
            halo(shift).start()
    @pl.when(g == 0)
    def _():
        pad[0] = jnp.zeros(pad.shape[1:], BF16)
        zh[:, 0] = jnp.zeros((2, 16, CIN), BF16)
        ch[:, :, 0] = jnp.zeros((2, 2, 8, CIN), F32)

    @pl.when(g == ngx - 1)
    def _():
        pad[3] = jnp.zeros(pad.shape[1:], BF16)
        zh[:, 3] = jnp.zeros((2, 16, CIN), BF16)
        ch[:, :, 2] = jnp.zeros((2, 2, 8, CIN), F32)

    for side, edge_at in ((0, 0), (1, ngy - 1)):
        @pl.when(a == edge_at)
        def _():
            pad[:, 17 * side] = jnp.zeros((4, 16, CIN), BF16)
            ch[:, side] = jnp.zeros((2, 3, 8, CIN), F32)

    for side, edge_at in ((0, 0), (1, ngz - 1)):
        @pl.when(b == edge_at)
        def _():
            zh[side] = jnp.zeros((4, 16, CIN), BF16)
            ch[side] = jnp.zeros((2, 3, 8, CIN), F32)

    for dz in range(3):
        slab[dz, 17 * half] = jnp.zeros((PLANE, C4), BF16)
    broad[:, 0:8] = jnp.zeros((18, 8, C4), F32)
    broad[:, 40:48] = jnp.zeros((18, 8, C4), F32)


    def shard_rows(first, piece):
        return w5b.at[3 * piece : 3 * piece + 3, pl.ds(pl.multiple_of(first + 48 * core, 16), 48), :]

    def shard_copy(piece):
        return pltpu.make_async_remote_copy(
            src_ref=shard_rows(0, piece), dst_ref=shard_rows(96, piece),
            send_sem=shard_send.at[0, piece], recv_sem=shard_recv.at[0, piece],
            device_id={"gy": other}, device_id_type=MESH,
        )

    def shard_relay(piece):
        return pltpu.make_async_remote_copy(
            src_ref=shard_rows(96, piece), dst_ref=shard_rows(96, piece),
            send_sem=shard_send.at[1, piece], recv_sem=shard_recv.at[1, piece],
            device_id={"gx": g + 1 - 2 * core}, device_id_type=MESH,
        )

    for load in w5_loads:
        load.wait()
    for piece in range(3):
        shard_copy(piece).start()

    def widen(x):
        for y in range(18):
            if not (x in (1, 2) and 1 <= y <= 16):
                row = (x * 18 + y) * 32 + 8
                wide[row : row + 16, :] = pad[x, y].astype(F32)
        for side, at in ((0, 7), (1, 24)):
            wide[pl.ds((x * 18 + 1) * 32 + at, 16, stride=32), :] = zh[side, x].astype(F32)
            for ys, y in ((0, 0), (1, 17)):
                source, row = ((0, 1), (1, 0), (1, 1), (2, 0))[x]
                first = (x * 18 + y) * 32 + at
                wide[first : first + 1, :] = ch[side, ys, source, row : row + 1, :]
        for y in range(18):
            row = (x * 18 + y) * 32
            left = wide[row + 7 : row + 23, :].astype(BF16)
            right = wide[row + 9 : row + 25, :].astype(BF16)
            taps[x, y * 16 : y * 16 + 16, :] = jnp.concatenate([left, pad[x, y], right], axis=-1)

    def around(x):
        return jnp.concatenate([taps[x, dy * 16 : dy * 16 + 256, :] for dy in range(3)], axis=-1)

    halo_wait([shift for shift in SHIFTS if shift[0] == 0])
    for db in (-1, 1):
        @pl.when(there(0, 0, db))
        def _():
            pl.semaphore_signal(known, inc=1, device_id=device(0, 0, db), device_id_type=MESH)
    for x in (1, 2):
        widen(x)
    w4_load.wait()
    span = 9 * CIN
    own = jnp.concatenate([around(1), around(2)], axis=-1)
    for x in (0, 1):
        first = (1 - x) * span
        hidden[x] = jnp.dot(own, w4b[first : first + 2 * span, :], preferred_element_type=F32)
    halo_wait([shift for shift in SHIFTS if shift[0]])
    for x in (0, 3):
        widen(x)
    tops = jnp.maximum(
        hidden[0] + jnp.dot(around(0), w4b[:span, :], preferred_element_type=F32),
        hidden[1] + jnp.dot(around(3), w4b[2 * span :, :], preferred_element_type=F32),
    )
    tops = jnp.max(tops.reshape(8, 2, 16, C4), axis=1).reshape(128, C4)
    for lanes in range(2):
        pool[lanes] = tops[:, lanes * 128 : lanes * 128 + 128]
    for lanes in range(2):
        tops = jnp.maximum(pool[lanes, pl.ds(0, 64, stride=2), :], pool[lanes, pl.ds(1, 64, stride=2), :])
        block[:, lanes * 128 : lanes * 128 + 128] = jnp.where(tops > 0, tops, 0.3 * tops).astype(BF16)

    mine = (a - 2 * half) * ngz + b
    offsets = [(di, db) for di in range(2) for db in range(ngz) if (di, db) != (0, 0)]

    def spread(di, db):
        number = di * ngz + db
        return pltpu.make_async_remote_copy(
            src_ref=block, dst_ref=blocks.at[mine], send_sem=block_send.at[number], recv_sem=block_recv.at[number],
            device_id={"gy": beside if di else a, "gz": lax.rem(b + db, ngz)}, device_id_type=MESH,
        )

    def rim_copy(t, db):
        return pltpu.make_async_remote_copy(
            src_ref=rim, dst_ref=rims.at[b], send_sem=rim_send.at[t, db], recv_sem=rim_recv.at[db],
            device_id={"gy": 2 * (1 - half) + t, "gz": lax.rem(b + db, ngz)}, device_id_type=MESH,
        )

    for at, first in ((1, 56), (2, 0)):
        @pl.when(a == at)
        def _():
            rim[...] = block[first : first + 8, :]

    pl.semaphore_wait(known, near(b, ngz) - 1)

    @pl.when(jnp.logical_or(a == 1, a == 2))
    def _():
        for db in (2, 1, 3, 0):
            for t in range(2):
                rim_copy(t, db).start()

    for di, db in ((1, 2), (0, 2), (1, 1), (1, 3), (0, 1), (0, 3), (1, 0)):
        spread(di, db).start()

    blocks[mine] = block[...]
    halo_sent()
    for piece in range(3):
        shard_copy(piece).wait_recv()
        shard_relay(piece).start()

    def spread_sent():
        for piece in range(3):
            shard_copy(piece).wait_send()
            shard_relay(piece).wait_send()
        for di, db in offsets:
            spread(di, db).wait_send()

        @pl.when(jnp.logical_or(a == 1, a == 2))
        def _():
            for t in range(2):
                for db in range(ngz):
                    rim_copy(t, db).wait_send()

    def lay(first, rows):
        for dz in range(3):
            for row in range(rows):
                slab[dz, first + row] = broad[first + row, 7 + dz : 39 + dz, :].astype(BF16)

    at = a - 2 * half
    taps_w5 = (((1,), (1,)), ((), ()))

    def settle(di, row):
        for db in range(ngz):
            if (di, db) != (0, 0):
                spread(di, db).wait_recv()
        for z in range(ngz):
            broad[pl.ds(1 + 8 * row, 8), 8 + 8 * z : 16 + 8 * z, :] = blocks[row * ngz + z].astype(F32).reshape(8, 8, C4)
        lay(1 + 8 * row, 8)

    def all_taps(numbers):
        return jnp.concatenate([w5b[number] for number in numbers], axis=-1)

    def rows_of(first, rows):
        return jnp.concatenate(
            [slab[dz, pl.ds(first + dy, rows)].reshape(rows * PLANE, C4) for dy in range(3) for dz in range(3)], axis=-1
        )

    settle(0, at)
    for dz in range(3):
        for row in (8 * at, 8 * at + 9):
            slab[dz, row] = jnp.zeros((PLANE, C4), BF16)
    for piece in range(3):
        shard_relay(piece).wait_recv()
    for part in range(2):
        early[128 * part : 128 * part + 128, :192] = lax.dot_general(
            rows_of(8 * at + 4 * part, 4), all_taps(range(9)), taps_w5, preferred_element_type=F32
        )
    settle(1, 1 - at)
    for db in range(ngz):
        rim_copy(0, db).wait_recv()
    for z in range(ngz):
        broad[17 * (1 - half), 8 + 8 * z : 16 + 8 * z, :] = rims[z].astype(F32)
    lay(17 * (1 - half), 1)

    parts = [(p, k) for p in (1, 0) for k in (0, 2, 1) if (p, k) != (0, 1)]

    def part_when(k, sender):
        if k == 1:
            return lambda f: f()
        if (k == 0) == sender:
            return pl.when(g < ngx - 1)
        return pl.when(g > 0)

    def part_copy(p, k, q):
        return pltpu.make_async_remote_copy(
            src_ref=sent.at[p, k, q], dst_ref=got.at[p, k, q], send_sem=part_send.at[p, k, q], recv_sem=part_recv.at[p, k, q],
            device_id={"gx": g + 1 - k, "gy": other if p else a}, device_id_type=MESH,
        )

    lane = lax.broadcasted_iota(jnp.int32, (64, 128), 1)

    def group(rows, j):
        tile, k = divmod(j, 4)
        moved = [
            pltpu.roll(rows[64 * u : 64 * u + 64, 128 * tile : 128 * tile + 128], (32 * (u - k)) % 128, axis=1)
            if u != k else rows[64 * u : 64 * u + 64, 128 * tile : 128 * tile + 128]
            for u in range(4)
        ]
        return jnp.where(lane < 64, jnp.where(lane < 32, moved[0], moved[1]), jnp.where(lane < 96, moved[2], moved[3]))

    def send_parts(total, slot):
        for p, k in parts:
            sent[p, k, slot] = group(total, 3 * p + k).astype(BF16)

            @part_when(k, True)
            def _():
                part_copy(p, k, slot).start()

        packed[0, slot] = group(total, 1)

    for row, first, dy in ((8 * at, 0, 0), (8 * at + 9, 224, 2)):
        early[first : first + PLANE, :192] += lax.dot_general(
            jnp.concatenate([slab[dz, row] for dz in range(3)], axis=-1),
            all_taps(range(3 * dy, 3 * dy + 3)),
            taps_w5, preferred_element_type=F32,
        )
    send_parts(early[...], 0)
    for part in range(2):
        late[128 * part : 128 * part + 128, :192] = lax.dot_general(
            rows_of(8 * (1 - at) + 4 * part, 4), all_taps(range(9)), taps_w5, preferred_element_type=F32
        )
    send_parts(late[...], 1)

    spread_sent()
    for slot in range(2):
        part_copy(1, 1, slot).wait_recv()
        packed[1, slot] = got[1, 1, slot].astype(F32)
    for k in (0, 2):
        @part_when(k, False)
        def _():
            for p in range(2):
                for slot in range(2):
                    part_copy(p, k, slot).wait_recv()
                    packed[p, slot] += got[p, k, slot].astype(F32)

    for p, place in ((0, half), (1, 1 - half)):
        for slot in range(2):
            out[place, at if p == slot else 1 - at] = packed[p, slot].astype(BF16)

    finish(9)


def body(sizes, volume, conv4_weight, conv5_weight):
    ngx, ngy, ngz = sizes
    any_space = pl.BlockSpec(memory_space=pl.ANY)
    packed = pl.pallas_call(
        functools.partial(kernel, sizes),
        out_shape=jax.ShapeDtypeStruct((2, 2, 64, 128), BF16),
        in_specs=[any_space] * 3,
        out_specs=pl.BlockSpec(memory_space=pltpu.VMEM),
        scratch_shapes=[
            pltpu.VMEM((4, 18, 16, CIN), BF16),
            pltpu.VMEM((4 * 18 * 32, CIN), F32),
            pltpu.VMEM((4, 18 * 16, 3 * CIN), BF16),
            pltpu.VMEM((27 * CIN, C4), BF16),
            pltpu.VMEM((9, 192, C4), BF16),
            pltpu.VMEM((2, 2, 16, CIN), BF16),
            pltpu.VMEM((2, 2, 8, CIN), F32),
            pltpu.VMEM((2, 4, 16, CIN), BF16),
            pltpu.VMEM((2, 2, 3, 8, CIN), F32),
            pltpu.VMEM((2, 256, C4), F32),
            pltpu.VMEM((256, 256), F32),
            pltpu.VMEM((256, 256), F32),
            pltpu.VMEM((2, 128, 128), F32),
            pltpu.VMEM((64, C4), BF16),
            pltpu.VMEM((2 * ngz, 64, C4), BF16),
            pltpu.VMEM((8, C4), BF16),
            pltpu.VMEM((ngz, 8, C4), BF16),
            pltpu.VMEM((3, 18, PLANE, C4), BF16),
            pltpu.VMEM((18, 48, C4), F32),
            pltpu.VMEM((2, 3, 2, 64, 128), BF16),
            pltpu.VMEM((2, 3, 2, 64, 128), BF16),
            pltpu.VMEM((2, 2, 64, 128), F32),
            pltpu.SemaphoreType.REGULAR,
            pltpu.SemaphoreType.DMA((5,)),
            pltpu.SemaphoreType.DMA((26,)),
            pltpu.SemaphoreType.DMA((26,)),
            pltpu.SemaphoreType.DMA((2 * ngz,)),
            pltpu.SemaphoreType.DMA((2 * ngz,)),
            pltpu.SemaphoreType.DMA((2, ngz)),
            pltpu.SemaphoreType.DMA((ngz,)),
            pltpu.SemaphoreType.DMA((2, 3, 2)),
            pltpu.SemaphoreType.DMA((2, 3, 2)),
            pltpu.SemaphoreType.DMA((2, 3)),
            pltpu.SemaphoreType.DMA((2, 3)),
        ],
        compiler_params=pltpu.CompilerParams(
            collective_id=0, has_side_effects=True, vmem_limit_bytes=40 * 1024 * 1024
        ),
    )(
        *(pltpu.with_memory_space_constraint(x, pltpu.HBM) for x in (volume, conv4_weight.reshape(27 * CIN, C4), jnp.swapaxes(conv5_weight, 3, 4).reshape(3, 9, FILTERS, C4))),
    )
    cells = packed.reshape(4, 2, PLANE, 4, FILTERS).transpose(0, 3, 1, 2, 4)
    return cells.reshape(1, PLANE, PLANE, FILTERS)


def solution(mesh):
    sizes = (mesh.shape["gx"], mesh.shape["gy"], mesh.shape["gz"])
    return jax.shard_map(
        functools.partial(body, sizes),
        mesh=mesh,
        in_specs=(
            P(("sample", "gx"), "gy", "gz", None),
            P(),
            P(None, None, None, None, ("gy", "gz")),
        ),
        out_specs=P(("sample", "gx"), None, None, ("gy", "gz")),
        check_vma=False,
    )
```

```python
import functools

import jax
import jax.numpy as jnp
from jax import lax
from jax.experimental import pallas as pl
from jax.experimental.pallas import tpu as pltpu
from jax.sharding import PartitionSpec as P

MESH = pl.DeviceIdType.MESH
BF16, F32 = jnp.bfloat16, jnp.float32
CIN, C4, FILTERS = 128, 256, 32
PLANE = 32
SHIFTS = [(i, j, k) for i in (-1, 0, 1) for j in (-1, 0, 1) for k in (-1, 0, 1) if (i, j, k) != (0, 0, 0)]


def kernel(
    sizes, v, w4, w5, out,
    pad, wide, taps, w4b, w5b, zs, yz, zh, ch, hidden, early, late, pool, block, blocks, rim, rims, slab, broad, sent, got, packed,
    known, load_sem, halo_send, halo_recv, block_send, block_recv, rim_send, rim_recv, part_send, part_recv, shard_send, shard_recv,
):
    ngx, ngy, ngz = sizes
    g, a, b = lax.axis_index("gx"), lax.axis_index("gy"), lax.axis_index("gz")
    half = lax.div(a, 2)
    core = lax.rem(g, 2)
    other = ngy - 1 - a
    beside = 4 * half + 1 - a

    def there(dg, da, db):
        ok = None
        for at, step, n in ((g, dg, ngx), (a, da, ngy), (b, db, ngz)):
            if step:
                fine = (at > 0) if step < 0 else (at < n - 1)
                ok = fine if ok is None else jnp.logical_and(ok, fine)
        return ok

    def device(dg, da, db):
        return {"gx": g + dg, "gy": a + da, "gz": b + db}

    own_load = pltpu.make_async_copy(v, pad.at[1:3, 1:17], load_sem.at[0])
    own_load.start()
    w4_load = pltpu.make_async_copy(w4, w4b, load_sem.at[1])
    w4_load.start()
    w5_loads = [
        pltpu.make_async_copy(w5.at[dx], w5b.at[:, dx * FILTERS : (dx + 1) * FILTERS, :], load_sem.at[2 + dx]) for dx in range(3)
    ]
    for load in w5_loads:
        load.start()

    barrier = pltpu.get_barrier_semaphore()
    for shift in sorted(SHIFTS, key=lambda shift: -sum(map(abs, shift))):
        @pl.when(there(*shift))
        def _():
            pl.semaphore_signal(barrier, inc=1, device_id=device(*shift), device_id_type=MESH)
    pl.semaphore_signal(barrier, inc=1, device_id={"gy": other}, device_id_type=MESH)

    def near(position, n):
        return 1 + (position > 0).astype(jnp.int32) + (position < n - 1).astype(jnp.int32)

    greeted = near(g, ngx) * near(a, ngy) * near(b, ngz)

    def finish(stage):
        if stage < 2:
            w4_load.wait()
        if stage < 2:
            for load in w5_loads:
                load.wait()
        if stage == 2:
            halo_wait([shift for shift in SHIFTS if shift[0]])
            w4_load.wait()
        if 2 <= stage < 4:
            halo_sent()
            for piece in range(3):
                shard_copy(piece).wait_send()
                shard_copy(piece).wait_recv()
        if stage == 4:
            spread_sent()
        if stage >= 5:
            for k in range(3):
                @part_when(k, True)
                def _():
                    some_of(sent.at[1, 1] if k == 1 else sent.at[:, k], part_send.at[k]).wait_send()

    yz[...] = jnp.zeros(yz.shape, F32)
    own_load.wait()
    for x in (1, 2):
        for y in range(1, 17):
            row = (x * 18 + y) * 32 + 8
            wide[row : row + 16, :] = pad[x, y].astype(F32)
    for side, z in ((0, 0), (1, 15)):
        for x in (0, 1):
            first = ((x + 1) * 18 + 1) * 32 + 8 + z
            column = wide[pl.ds(first, 16, stride=32), :]
            zs[side, x] = column.astype(BF16)
            for ys, y in ((0, 0), (1, 15)):
                yz[side, ys, x : x + 1, :] = column[y : y + 1]

    pl.semaphore_wait(barrier, greeted)

    def halo(shift):
        dg, da, db = shift
        x = {-1: 0, 1: 1}.get(dg)
        px = {-1: 3, 1: 0}.get(dg)
        y = {-1: 0, 1: 15}.get(da)
        py = {-1: 17, 1: 0}.get(da)
        s = {-1: 0, 1: 1}.get(db)
        if db == 0:
            if da == 0:
                src, dst = pad.at[x + 1, 1:17], pad.at[px, 1:17]
            elif dg == 0:
                src, dst = pad.at[1:3, y + 1], pad.at[1:3, py]
            else:
                src, dst = pad.at[x + 1, y + 1], pad.at[px, py]
        elif da == 0:
            if dg == 0:
                src, dst = zs.at[s], zh.at[1 - s, 1:3]
            else:
                src, dst = zs.at[s, x], zh.at[1 - s, px]
        else:
            ys = {-1: 0, 1: 1}[da]
            src, dst = yz.at[s, ys], ch.at[1 - s, 1 - ys, {-1: 2, 0: 1, 1: 0}[dg]]
        number = SHIFTS.index(shift)
        return pltpu.make_async_remote_copy(
            src_ref=src, dst_ref=dst, send_sem=halo_send.at[number], recv_sem=halo_recv.at[number],
            device_id=device(*shift), device_id_type=MESH,
        )

    def halo_sent():
        for shift in SHIFTS:
            @pl.when(there(*shift))
            def _():
                halo(shift).wait_send()

    def halo_wait(shifts):
        for shift in shifts:
            @pl.when(there(*(-i for i in shift)))
            def _():
                halo(shift).wait_recv()

    for shift in sorted(SHIFTS, key=lambda shift: (shift[0] != 0, -sum(map(abs, shift)))):
        @pl.when(there(*shift))
        def _():
            halo(shift).start()
    @pl.when(g == 0)
    def _():
        pad[0] = jnp.zeros(pad.shape[1:], BF16)
        zh[:, 0] = jnp.zeros((2, 16, CIN), BF16)
        ch[:, :, 0] = jnp.zeros((2, 2, 8, CIN), F32)

    @pl.when(g == ngx - 1)
    def _():
        pad[3] = jnp.zeros(pad.shape[1:], BF16)
        zh[:, 3] = jnp.zeros((2, 16, CIN), BF16)
        ch[:, :, 2] = jnp.zeros((2, 2, 8, CIN), F32)

    for side, edge_at in ((0, 0), (1, ngy - 1)):
        @pl.when(a == edge_at)
        def _():
            pad[:, 17 * side] = jnp.zeros((4, 16, CIN), BF16)
            ch[:, side] = jnp.zeros((2, 3, 8, CIN), F32)

    for side, edge_at in ((0, 0), (1, ngz - 1)):
        @pl.when(b == edge_at)
        def _():
            zh[side] = jnp.zeros((4, 16, CIN), BF16)
            ch[side] = jnp.zeros((2, 3, 8, CIN), F32)

    for dz in range(3):
        slab[dz, 17 * half] = jnp.zeros((PLANE, C4), BF16)
    broad[:, 0:8] = jnp.zeros((18, 8, C4), F32)
    broad[:, 40:48] = jnp.zeros((18, 8, C4), F32)


    def shard_rows(first, piece):
        return w5b.at[3 * piece : 3 * piece + 3, pl.ds(pl.multiple_of(first + 48 * core, 16), 48), :]

    def shard_copy(piece):
        return pltpu.make_async_remote_copy(
            src_ref=shard_rows(0, piece), dst_ref=shard_rows(96, piece),
            send_sem=shard_send.at[0, piece], recv_sem=shard_recv.at[0, piece],
            device_id={"gy": other}, device_id_type=MESH,
        )

    def shard_relay(piece):
        return pltpu.make_async_remote_copy(
            src_ref=shard_rows(96, piece), dst_ref=shard_rows(96, piece),
            send_sem=shard_send.at[1, piece], recv_sem=shard_recv.at[1, piece],
            device_id={"gx": g + 1 - 2 * core}, device_id_type=MESH,
        )

    for load in w5_loads:
        load.wait()
    for piece in range(3):
        shard_copy(piece).start()

    def widen(x):
        for y in range(18):
            if not (x in (1, 2) and 1 <= y <= 16):
                row = (x * 18 + y) * 32 + 8
                wide[row : row + 16, :] = pad[x, y].astype(F32)
        for side, at in ((0, 7), (1, 24)):
            wide[pl.ds((x * 18 + 1) * 32 + at, 16, stride=32), :] = zh[side, x].astype(F32)
            for ys, y in ((0, 0), (1, 17)):
                source, row = ((0, 1), (1, 0), (1, 1), (2, 0))[x]
                first = (x * 18 + y) * 32 + at
                wide[first : first + 1, :] = ch[side, ys, source, row : row + 1, :]
        for y in range(18):
            row = (x * 18 + y) * 32
            left = wide[row + 7 : row + 23, :].astype(BF16)
            right = wide[row + 9 : row + 25, :].astype(BF16)
            taps[x, y * 16 : y * 16 + 16, :] = jnp.concatenate([left, pad[x, y], right], axis=-1)

    def around(x):
        return jnp.concatenate([taps[x, dy * 16 : dy * 16 + 256, :] for dy in range(3)], axis=-1)

    halo_wait([shift for shift in SHIFTS if shift[0] == 0])
    for db in (-1, 1):
        @pl.when(there(0, 0, db))
        def _():
            pl.semaphore_signal(known, inc=1, device_id=device(0, 0, db), device_id_type=MESH)
    for x in (1, 2):
        widen(x)
    w4_load.wait()
    span = 9 * CIN
    own = jnp.concatenate([around(1), around(2)], axis=-1)
    for x in (0, 1):
        first = (1 - x) * span
        hidden[x] = jnp.dot(own, w4b[first : first + 2 * span, :], preferred_element_type=F32)
    halo_wait([shift for shift in SHIFTS if shift[0]])
    for x in (0, 3):
        widen(x)
    tops = jnp.maximum(
        hidden[0] + jnp.dot(around(0), w4b[:span, :], preferred_element_type=F32),
        hidden[1] + jnp.dot(around(3), w4b[2 * span :, :], preferred_element_type=F32),
    )
    tops = jnp.max(tops.reshape(8, 2, 16, C4), axis=1).reshape(128, C4)
    for lanes in range(2):
        pool[lanes] = tops[:, lanes * 128 : lanes * 128 + 128]
    for lanes in range(2):
        tops = jnp.maximum(pool[lanes, pl.ds(0, 64, stride=2), :], pool[lanes, pl.ds(1, 64, stride=2), :])
        block[:, lanes * 128 : lanes * 128 + 128] = jnp.where(tops > 0, tops, 0.3 * tops).astype(BF16)

    mine = (a - 2 * half) * ngz + b
    offsets = [(di, db) for di in range(2) for db in range(ngz) if (di, db) != (0, 0)]

    def spread(di, db):
        return pltpu.make_async_remote_copy(
            src_ref=block, dst_ref=blocks.at[mine], send_sem=block_send, recv_sem=block_recv.at[di],
            device_id={"gy": beside if di else a, "gz": lax.rem(b + db, ngz)}, device_id_type=MESH,
        )

    def some_of(ref, sem):
        return pltpu.make_async_remote_copy(
            src_ref=ref, dst_ref=ref, send_sem=sem, recv_sem=sem, device_id={"gz": lax.rem(b + 1, ngz)}, device_id_type=MESH
        )

    def rim_copy(t, db):
        return pltpu.make_async_remote_copy(
            src_ref=rim, dst_ref=rims.at[b], send_sem=rim_send, recv_sem=rim_recv,
            device_id={"gy": 2 * (1 - half) + t, "gz": lax.rem(b + db, ngz)}, device_id_type=MESH,
        )

    for at, first in ((1, 56), (2, 0)):
        @pl.when(a == at)
        def _():
            rim[...] = block[first : first + 8, :]

    pl.semaphore_wait(known, near(b, ngz) - 1)

    @pl.when(jnp.logical_or(a == 1, a == 2))
    def _():
        for db in (2, 1, 3, 0):
            for t in range(2):
                rim_copy(t, db).start()

    for di, db in ((1, 2), (0, 2), (1, 1), (1, 3), (0, 1), (0, 3), (1, 0)):
        spread(di, db).start()

    blocks[mine] = block[...]
    halo_sent()
    for piece in range(3):
        shard_copy(piece).wait_recv()
        shard_relay(piece).start()

    def spread_sent():
        for piece in range(3):
            shard_copy(piece).wait_send()
            shard_relay(piece).wait_send()
        some_of(blocks.at[0:7], block_send).wait_send()

        @pl.when(jnp.logical_or(a == 1, a == 2))
        def _():
            some_of(block, rim_send).wait_send()

    def lay(first, rows):
        for dz in range(3):
            for row in range(rows):
                slab[dz, first + row] = broad[first + row, 7 + dz : 39 + dz, :].astype(BF16)

    at = a - 2 * half
    taps_w5 = (((1,), (1,)), ((), ()))

    def settle(di, row):
        some_of(blocks.at[pl.ds(4 * row, 4)] if di else blocks.at[0:3], block_recv.at[di]).wait_recv()
        for z in range(ngz):
            broad[pl.ds(1 + 8 * row, 8), 8 + 8 * z : 16 + 8 * z, :] = blocks[row * ngz + z].astype(F32).reshape(8, 8, C4)
        lay(1 + 8 * row, 8)

    def all_taps(numbers):
        return jnp.concatenate([w5b[number] for number in numbers], axis=-1)

    def rows_of(first, rows):
        return jnp.concatenate(
            [slab[dz, pl.ds(first + dy, rows)].reshape(rows * PLANE, C4) for dy in range(3) for dz in range(3)], axis=-1
        )

    settle(0, at)
    for dz in range(3):
        for row in (8 * at, 8 * at + 9):
            slab[dz, row] = jnp.zeros((PLANE, C4), BF16)
    for piece in range(3):
        shard_relay(piece).wait_recv()
    for part in range(2):
        early[128 * part : 128 * part + 128, :192] = lax.dot_general(
            rows_of(8 * at + 4 * part, 4), all_taps(range(9)), taps_w5, preferred_element_type=F32
        )
    settle(1, 1 - at)
    some_of(rims, rim_recv).wait_recv()
    for z in range(ngz):
        broad[17 * (1 - half), 8 + 8 * z : 16 + 8 * z, :] = rims[z].astype(F32)
    lay(17 * (1 - half), 1)

    parts = [(p, k) for p in (1, 0) for k in (0, 2, 1) if (p, k) != (0, 1)]

    def part_when(k, sender):
        if k == 1:
            return lambda f: f()
        if (k == 0) == sender:
            return pl.when(g < ngx - 1)
        return pl.when(g > 0)

    def part_copy(p, k, q):
        return pltpu.make_async_remote_copy(
            src_ref=sent.at[p, k, q], dst_ref=got.at[p, k, q], send_sem=part_send.at[k], recv_sem=part_recv.at[k],
            device_id={"gx": g + 1 - k, "gy": other if p else a}, device_id_type=MESH,
        )

    lane = lax.broadcasted_iota(jnp.int32, (64, 128), 1)

    def group(rows, j):
        tile, k = divmod(j, 4)
        moved = [
            pltpu.roll(rows[64 * u : 64 * u + 64, 128 * tile : 128 * tile + 128], (32 * (u - k)) % 128, axis=1)
            if u != k else rows[64 * u : 64 * u + 64, 128 * tile : 128 * tile + 128]
            for u in range(4)
        ]
        return jnp.where(lane < 64, jnp.where(lane < 32, moved[0], moved[1]), jnp.where(lane < 96, moved[2], moved[3]))

    def send_parts(total, slot):
        for p, k in parts:
            sent[p, k, slot] = group(total, 3 * p + k).astype(BF16)

            @part_when(k, True)
            def _():
                part_copy(p, k, slot).start()

        packed[0, slot] = group(total, 1)

    for row, first, dy in ((8 * at, 0, 0), (8 * at + 9, 224, 2)):
        early[first : first + PLANE, :192] += lax.dot_general(
            jnp.concatenate([slab[dz, row] for dz in range(3)], axis=-1),
            all_taps(range(3 * dy, 3 * dy + 3)),
            taps_w5, preferred_element_type=F32,
        )
    send_parts(early[...], 0)
    for part in range(2):
        late[128 * part : 128 * part + 128, :192] = lax.dot_general(
            rows_of(8 * (1 - at) + 4 * part, 4), all_taps(range(9)), taps_w5, preferred_element_type=F32
        )
    send_parts(late[...], 1)

    spread_sent()
    some_of(got.at[1, 1], part_recv.at[1]).wait_recv()
    packed[1] = got[1, 1].astype(F32)
    for k in (0, 2):
        @part_when(k, False)
        def _():
            some_of(got.at[:, k], part_recv.at[k]).wait_recv()
            packed[...] += got[:, k].astype(F32)

    for p, place in ((0, half), (1, 1 - half)):
        for slot in range(2):
            out[place, at if p == slot else 1 - at] = packed[p, slot].astype(BF16)

    finish(9)


def body(sizes, volume, conv4_weight, conv5_weight):
    ngx, ngy, ngz = sizes
    any_space = pl.BlockSpec(memory_space=pl.ANY)
    packed = pl.pallas_call(
        functools.partial(kernel, sizes),
        out_shape=jax.ShapeDtypeStruct((2, 2, 64, 128), BF16),
        in_specs=[any_space] * 3,
        out_specs=pl.BlockSpec(memory_space=pltpu.VMEM),
        scratch_shapes=[
            pltpu.VMEM((4, 18, 16, CIN), BF16),
            pltpu.VMEM((4 * 18 * 32, CIN), F32),
            pltpu.VMEM((4, 18 * 16, 3 * CIN), BF16),
            pltpu.VMEM((27 * CIN, C4), BF16),
            pltpu.VMEM((9, 192, C4), BF16),
            pltpu.VMEM((2, 2, 16, CIN), BF16),
            pltpu.VMEM((2, 2, 8, CIN), F32),
            pltpu.VMEM((2, 4, 16, CIN), BF16),
            pltpu.VMEM((2, 2, 3, 8, CIN), F32),
            pltpu.VMEM((2, 256, C4), F32),
            pltpu.VMEM((256, 256), F32),
            pltpu.VMEM((256, 256), F32),
            pltpu.VMEM((2, 128, 128), F32),
            pltpu.VMEM((64, C4), BF16),
            pltpu.VMEM((2 * ngz, 64, C4), BF16),
            pltpu.VMEM((8, C4), BF16),
            pltpu.VMEM((ngz, 8, C4), BF16),
            pltpu.VMEM((3, 18, PLANE, C4), BF16),
            pltpu.VMEM((18, 48, C4), F32),
            pltpu.VMEM((2, 3, 2, 64, 128), BF16),
            pltpu.VMEM((2, 3, 2, 64, 128), BF16),
            pltpu.VMEM((2, 2, 64, 128), F32),
            pltpu.SemaphoreType.REGULAR,
            pltpu.SemaphoreType.DMA((5,)),
            pltpu.SemaphoreType.DMA((26,)),
            pltpu.SemaphoreType.DMA((26,)),
            pltpu.SemaphoreType.DMA,
            pltpu.SemaphoreType.DMA((2,)),
            pltpu.SemaphoreType.DMA,
            pltpu.SemaphoreType.DMA,
            pltpu.SemaphoreType.DMA((3,)),
            pltpu.SemaphoreType.DMA((3,)),
            pltpu.SemaphoreType.DMA((2, 3)),
            pltpu.SemaphoreType.DMA((2, 3)),
        ],
        compiler_params=pltpu.CompilerParams(
            collective_id=0, has_side_effects=True, vmem_limit_bytes=40 * 1024 * 1024
        ),
    )(
        *(pltpu.with_memory_space_constraint(x, pltpu.HBM) for x in (volume, conv4_weight.reshape(27 * CIN, C4), jnp.swapaxes(conv5_weight, 3, 4).reshape(3, 9, FILTERS, C4))),
    )
    cells = packed.reshape(4, 2, PLANE, 4, FILTERS).transpose(0, 3, 1, 2, 4)
    return cells.reshape(1, PLANE, PLANE, FILTERS)


def solution(mesh):
    sizes = (mesh.shape["gx"], mesh.shape["gy"], mesh.shape["gz"])
    return jax.shard_map(
        functools.partial(body, sizes),
        mesh=mesh,
        in_specs=(
            P(("sample", "gx"), "gy", "gz", None),
            P(),
            P(None, None, None, None, ("gy", "gz")),
        ),
        out_specs=P(("sample", "gx"), None, None, ("gy", "gz")),
        check_vma=False,
    )
```

```python
import functools

import jax
import jax.numpy as jnp
from jax import lax
from jax.experimental import pallas as pl
from jax.experimental.pallas import tpu as pltpu
from jax.sharding import PartitionSpec as P

MESH = pl.DeviceIdType.MESH
BF16, F32 = jnp.bfloat16, jnp.float32
CIN, C4, FILTERS = 128, 256, 32
PLANE = 32
SHIFTS = [(i, j, k) for i in (-1, 0, 1) for j in (-1, 0, 1) for k in (-1, 0, 1) if (i, j, k) != (0, 0, 0)]


def kernel(
    sizes, v, w4, w5, out,
    pad, wide, taps, w4b, w5b, zs, yz, zh, ch, hidden, early, late, pool, block, blocks, rim, rims, slab, broad, sent, got, packed,
    known, load_sem, halo_send, halo_recv, block_send, block_recv, rim_send, rim_recv, part_send, part_recv, shard_send, shard_recv,
):
    ngx, ngy, ngz = sizes
    g, a, b = lax.axis_index("gx"), lax.axis_index("gy"), lax.axis_index("gz")
    half = lax.div(a, 2)
    core = lax.rem(g, 2)
    other = ngy - 1 - a
    beside = 4 * half + 1 - a

    def there(dg, da, db):
        ok = None
        for at, step, n in ((g, dg, ngx), (a, da, ngy), (b, db, ngz)):
            if step:
                fine = (at > 0) if step < 0 else (at < n - 1)
                ok = fine if ok is None else jnp.logical_and(ok, fine)
        return ok

    def device(dg, da, db):
        return {"gx": g + dg, "gy": a + da, "gz": b + db}

    own_load = pltpu.make_async_copy(v, pad.at[1:3, 1:17], load_sem.at[0])
    own_load.start()
    w4_load = pltpu.make_async_copy(w4, w4b, load_sem.at[1])
    w4_load.start()
    w5_loads = [
        pltpu.make_async_copy(w5.at[dx], w5b.at[:, dx * FILTERS : (dx + 1) * FILTERS, :], load_sem.at[2 + dx]) for dx in range(3)
    ]
    for load in w5_loads:
        load.start()

    barrier = pltpu.get_barrier_semaphore()
    for shift in sorted(SHIFTS, key=lambda shift: -sum(map(abs, shift))):
        @pl.when(there(*shift))
        def _():
            pl.semaphore_signal(barrier, inc=1, device_id=device(*shift), device_id_type=MESH)
    pl.semaphore_signal(barrier, inc=1, device_id={"gy": other}, device_id_type=MESH)

    def near(position, n):
        return 1 + (position > 0).astype(jnp.int32) + (position < n - 1).astype(jnp.int32)

    greeted = near(g, ngx) * near(a, ngy) * near(b, ngz)

    def finish(stage):
        if stage < 2:
            w4_load.wait()
        if stage < 2:
            for load in w5_loads:
                load.wait()
        if stage == 2:
            halo_wait([shift for shift in SHIFTS if shift[0]])
            w4_load.wait()
        if 2 <= stage < 4:
            halo_sent()
            for piece in range(3):
                shard_copy(piece).wait_send()
                shard_copy(piece).wait_recv()
        if stage == 4:
            spread_sent()
        if stage >= 5:
            for k in range(3):
                @part_when(k, True)
                def _():
                    some_of(sent.at[1, 1] if k == 1 else sent.at[:, k], part_send.at[k]).wait_send()

    yz[...] = jnp.zeros(yz.shape, F32)
    own_load.wait()
    for x in (1, 2):
        for y in range(1, 17):
            row = (x * 18 + y) * 32 + 8
            wide[row : row + 16, :] = pad[x, y].astype(F32)
    for side, z in ((0, 0), (1, 15)):
        for x in (0, 1):
            first = ((x + 1) * 18 + 1) * 32 + 8 + z
            column = wide[pl.ds(first, 16, stride=32), :]
            zs[side, x] = column.astype(BF16)
            for ys, y in ((0, 0), (1, 15)):
                yz[side, ys, x : x + 1, :] = column[y : y + 1]

    pl.semaphore_wait(barrier, greeted)

    def halo(shift):
        dg, da, db = shift
        x = {-1: 0, 1: 1}.get(dg)
        px = {-1: 3, 1: 0}.get(dg)
        y = {-1: 0, 1: 15}.get(da)
        py = {-1: 17, 1: 0}.get(da)
        s = {-1: 0, 1: 1}.get(db)
        if db == 0:
            if da == 0:
                src, dst = pad.at[x + 1, 1:17], pad.at[px, 1:17]
            elif dg == 0:
                src, dst = pad.at[1:3, y + 1], pad.at[1:3, py]
            else:
                src, dst = pad.at[x + 1, y + 1], pad.at[px, py]
        elif da == 0:
            if dg == 0:
                src, dst = zs.at[s], zh.at[1 - s, 1:3]
            else:
                src, dst = zs.at[s, x], zh.at[1 - s, px]
        else:
            ys = {-1: 0, 1: 1}[da]
            src, dst = yz.at[s, ys], ch.at[1 - s, 1 - ys, {-1: 2, 0: 1, 1: 0}[dg]]
        number = SHIFTS.index(shift)
        return pltpu.make_async_remote_copy(
            src_ref=src, dst_ref=dst, send_sem=halo_send.at[number], recv_sem=halo_recv.at[number],
            device_id=device(*shift), device_id_type=MESH,
        )

    def halo_sent():
        for shift in SHIFTS:
            @pl.when(there(*shift))
            def _():
                halo(shift).wait_send()

    def halo_wait(shifts):
        for shift in shifts:
            @pl.when(there(*(-i for i in shift)))
            def _():
                halo(shift).wait_recv()

    for shift in sorted(SHIFTS, key=lambda shift: (shift[0] != 0, -sum(map(abs, shift)))):
        @pl.when(there(*shift))
        def _():
            halo(shift).start()
    @pl.when(g == 0)
    def _():
        pad[0] = jnp.zeros(pad.shape[1:], BF16)
        zh[:, 0] = jnp.zeros((2, 16, CIN), BF16)
        ch[:, :, 0] = jnp.zeros((2, 2, 8, CIN), F32)

    @pl.when(g == ngx - 1)
    def _():
        pad[3] = jnp.zeros(pad.shape[1:], BF16)
        zh[:, 3] = jnp.zeros((2, 16, CIN), BF16)
        ch[:, :, 2] = jnp.zeros((2, 2, 8, CIN), F32)

    for side, edge_at in ((0, 0), (1, ngy - 1)):
        @pl.when(a == edge_at)
        def _():
            pad[:, 17 * side] = jnp.zeros((4, 16, CIN), BF16)
            ch[:, side] = jnp.zeros((2, 3, 8, CIN), F32)

    for side, edge_at in ((0, 0), (1, ngz - 1)):
        @pl.when(b == edge_at)
        def _():
            zh[side] = jnp.zeros((4, 16, CIN), BF16)
            ch[side] = jnp.zeros((2, 3, 8, CIN), F32)

    for dz in range(3):
        slab[dz, 17 * half] = jnp.zeros((PLANE, C4), BF16)
    broad[:, 0:8] = jnp.zeros((18, 8, C4), F32)
    broad[:, 40:48] = jnp.zeros((18, 8, C4), F32)


    def shard_rows(first, piece):
        return w5b.at[3 * piece : 3 * piece + 3, pl.ds(pl.multiple_of(first + 48 * core, 16), 48), :]

    def shard_copy(piece):
        return pltpu.make_async_remote_copy(
            src_ref=shard_rows(0, piece), dst_ref=shard_rows(96, piece),
            send_sem=shard_send.at[0], recv_sem=shard_recv.at[0, piece],
            device_id={"gy": other}, device_id_type=MESH,
        )

    def shard_relay(piece):
        return pltpu.make_async_remote_copy(
            src_ref=shard_rows(96, piece), dst_ref=shard_rows(96, piece),
            send_sem=shard_send.at[1], recv_sem=shard_recv.at[1, 0],
            device_id={"gx": g + 1 - 2 * core}, device_id_type=MESH,
        )

    for load in w5_loads:
        load.wait()
    for piece in range(3):
        shard_copy(piece).start()

    def widen(x):
        for y in range(18):
            if not (x in (1, 2) and 1 <= y <= 16):
                row = (x * 18 + y) * 32 + 8
                wide[row : row + 16, :] = pad[x, y].astype(F32)
        for side, at in ((0, 7), (1, 24)):
            wide[pl.ds((x * 18 + 1) * 32 + at, 16, stride=32), :] = zh[side, x].astype(F32)
            for ys, y in ((0, 0), (1, 17)):
                source, row = ((0, 1), (1, 0), (1, 1), (2, 0))[x]
                first = (x * 18 + y) * 32 + at
                wide[first : first + 1, :] = ch[side, ys, source, row : row + 1, :]
        for y in range(18):
            row = (x * 18 + y) * 32
            left = wide[row + 7 : row + 23, :].astype(BF16)
            right = wide[row + 9 : row + 25, :].astype(BF16)
            taps[x, y * 16 : y * 16 + 16, :] = jnp.concatenate([left, pad[x, y], right], axis=-1)

    def around(x):
        return jnp.concatenate([taps[x, dy * 16 : dy * 16 + 256, :] for dy in range(3)], axis=-1)

    halo_wait([shift for shift in SHIFTS if shift[0] == 0])
    for db in (-1, 1):
        @pl.when(there(0, 0, db))
        def _():
            pl.semaphore_signal(known, inc=1, device_id=device(0, 0, db), device_id_type=MESH)
    for x in (1, 2):
        widen(x)
    w4_load.wait()
    span = 9 * CIN
    own = jnp.concatenate([around(1), around(2)], axis=-1)
    for x in (0, 1):
        first = (1 - x) * span
        hidden[x] = jnp.dot(own, w4b[first : first + 2 * span, :], preferred_element_type=F32)
    halo_wait([shift for shift in SHIFTS if shift[0]])
    for x in (0, 3):
        widen(x)
    tops = jnp.maximum(
        hidden[0] + jnp.dot(around(0), w4b[:span, :], preferred_element_type=F32),
        hidden[1] + jnp.dot(around(3), w4b[2 * span :, :], preferred_element_type=F32),
    )
    tops = jnp.max(tops.reshape(8, 2, 16, C4), axis=1).reshape(128, C4)
    for lanes in range(2):
        pool[lanes] = tops[:, lanes * 128 : lanes * 128 + 128]
    for lanes in range(2):
        tops = jnp.maximum(pool[lanes, pl.ds(0, 64, stride=2), :], pool[lanes, pl.ds(1, 64, stride=2), :])
        block[:, lanes * 128 : lanes * 128 + 128] = jnp.where(tops > 0, tops, 0.3 * tops).astype(BF16)

    mine = (a - 2 * half) * ngz + b
    offsets = [(di, db) for di in range(2) for db in range(ngz) if (di, db) != (0, 0)]

    def spread(di, db):
        return pltpu.make_async_remote_copy(
            src_ref=block, dst_ref=blocks.at[mine], send_sem=block_send, recv_sem=block_recv.at[di],
            device_id={"gy": beside if di else a, "gz": lax.rem(b + db, ngz)}, device_id_type=MESH,
        )

    def some_of(ref, sem):
        return pltpu.make_async_remote_copy(
            src_ref=ref, dst_ref=ref, send_sem=sem, recv_sem=sem, device_id={"gz": lax.rem(b + 1, ngz)}, device_id_type=MESH
        )

    def rim_copy(t, db):
        return pltpu.make_async_remote_copy(
            src_ref=rim, dst_ref=rims.at[b], send_sem=rim_send, recv_sem=rim_recv,
            device_id={"gy": 2 * (1 - half) + t, "gz": lax.rem(b + db, ngz)}, device_id_type=MESH,
        )

    for at, first in ((1, 56), (2, 0)):
        @pl.when(a == at)
        def _():
            rim[...] = block[first : first + 8, :]

    pl.semaphore_wait(known, near(b, ngz) - 1)

    @pl.when(jnp.logical_or(a == 1, a == 2))
    def _():
        for db in (2, 1, 3, 0):
            for t in range(2):
                rim_copy(t, db).start()

    for di, db in ((1, 2), (0, 2), (1, 1), (1, 3), (0, 1), (0, 3), (1, 0)):
        spread(di, db).start()

    blocks[mine] = block[...]
    halo_sent()
    for piece in range(3):
        shard_copy(piece).wait_recv()
        shard_relay(piece).start()

    def spread_sent():
        for kind in range(2):
            some_of(w5b.at[:, 0:48], shard_send.at[kind]).wait_send()
        some_of(blocks.at[0:7], block_send).wait_send()

        @pl.when(jnp.logical_or(a == 1, a == 2))
        def _():
            some_of(block, rim_send).wait_send()

    def lay(first, rows):
        for dz in range(3):
            for row in range(rows):
                slab[dz, first + row] = broad[first + row, 7 + dz : 39 + dz, :].astype(BF16)

    at = a - 2 * half
    taps_w5 = (((1,), (1,)), ((), ()))

    def settle(di, row):
        some_of(blocks.at[pl.ds(4 * row, 4)] if di else blocks.at[0:3], block_recv.at[di]).wait_recv()
        for z in range(ngz):
            broad[pl.ds(1 + 8 * row, 8), 8 + 8 * z : 16 + 8 * z, :] = blocks[row * ngz + z].astype(F32).reshape(8, 8, C4)
        lay(1 + 8 * row, 8)

    def all_taps(numbers):
        return jnp.concatenate([w5b[number] for number in numbers], axis=-1)

    def rows_of(first, rows):
        return jnp.concatenate(
            [slab[dz, pl.ds(first + dy, rows)].reshape(rows * PLANE, C4) for dy in range(3) for dz in range(3)], axis=-1
        )

    settle(0, at)
    for dz in range(3):
        for row in (8 * at, 8 * at + 9):
            slab[dz, row] = jnp.zeros((PLANE, C4), BF16)
    some_of(w5b.at[:, 0:48], shard_recv.at[1, 0]).wait_recv()
    for part in range(2):
        early[128 * part : 128 * part + 128, :192] = lax.dot_general(
            rows_of(8 * at + 4 * part, 4), all_taps(range(9)), taps_w5, preferred_element_type=F32
        )
    settle(1, 1 - at)
    some_of(rims, rim_recv).wait_recv()
    for z in range(ngz):
        broad[17 * (1 - half), 8 + 8 * z : 16 + 8 * z, :] = rims[z].astype(F32)
    lay(17 * (1 - half), 1)

    parts = [(p, k) for p in (1, 0) for k in (0, 2, 1) if (p, k) != (0, 1)]

    def part_when(k, sender):
        if k == 1:
            return lambda f: f()
        if (k == 0) == sender:
            return pl.when(g < ngx - 1)
        return pl.when(g > 0)

    def part_copy(p, k, q):
        return pltpu.make_async_remote_copy(
            src_ref=sent.at[p, k, q], dst_ref=got.at[p, k, q], send_sem=part_send.at[k], recv_sem=part_recv.at[k],
            device_id={"gx": g + 1 - k, "gy": other if p else a}, device_id_type=MESH,
        )

    lane = lax.broadcasted_iota(jnp.int32, (64, 128), 1)

    def group(rows, j):
        tile, k = divmod(j, 4)
        moved = [
            pltpu.roll(rows[64 * u : 64 * u + 64, 128 * tile : 128 * tile + 128], (32 * (u - k)) % 128, axis=1)
            if u != k else rows[64 * u : 64 * u + 64, 128 * tile : 128 * tile + 128]
            for u in range(4)
        ]
        return jnp.where(lane < 64, jnp.where(lane < 32, moved[0], moved[1]), jnp.where(lane < 96, moved[2], moved[3]))

    def send_parts(total, slot):
        for p, k in parts:
            sent[p, k, slot] = group(total, 3 * p + k).astype(BF16)

            @part_when(k, True)
            def _():
                part_copy(p, k, slot).start()

        packed[0, slot] = group(total, 1)

    for row, first, dy in ((8 * at, 0, 0), (8 * at + 9, 224, 2)):
        early[first : first + PLANE, :192] += lax.dot_general(
            jnp.concatenate([slab[dz, row] for dz in range(3)], axis=-1),
            all_taps(range(3 * dy, 3 * dy + 3)),
            taps_w5, preferred_element_type=F32,
        )
    send_parts(early[...], 0)
    for part in range(2):
        late[128 * part : 128 * part + 128, :192] = lax.dot_general(
            rows_of(8 * (1 - at) + 4 * part, 4), all_taps(range(9)), taps_w5, preferred_element_type=F32
        )
    send_parts(late[...], 1)

    spread_sent()
    some_of(got.at[1, 1], part_recv.at[1]).wait_recv()
    packed[1] = got[1, 1].astype(F32)
    for k in (0, 2):
        @part_when(k, False)
        def _():
            some_of(got.at[:, k], part_recv.at[k]).wait_recv()
            packed[...] += got[:, k].astype(F32)

    for p, place in ((0, half), (1, 1 - half)):
        for slot in range(2):
            out[place, at if p == slot else 1 - at] = packed[p, slot].astype(BF16)

    finish(9)


def body(sizes, volume, conv4_weight, conv5_weight):
    ngx, ngy, ngz = sizes
    any_space = pl.BlockSpec(memory_space=pl.ANY)
    packed = pl.pallas_call(
        functools.partial(kernel, sizes),
        out_shape=jax.ShapeDtypeStruct((2, 2, 64, 128), BF16),
        in_specs=[any_space] * 3,
        out_specs=pl.BlockSpec(memory_space=pltpu.VMEM),
        scratch_shapes=[
            pltpu.VMEM((4, 18, 16, CIN), BF16),
            pltpu.VMEM((4 * 18 * 32, CIN), F32),
            pltpu.VMEM((4, 18 * 16, 3 * CIN), BF16),
            pltpu.VMEM((27 * CIN, C4), BF16),
            pltpu.VMEM((9, 192, C4), BF16),
            pltpu.VMEM((2, 2, 16, CIN), BF16),
            pltpu.VMEM((2, 2, 8, CIN), F32),
            pltpu.VMEM((2, 4, 16, CIN), BF16),
            pltpu.VMEM((2, 2, 3, 8, CIN), F32),
            pltpu.VMEM((2, 256, C4), F32),
            pltpu.VMEM((256, 256), F32),
            pltpu.VMEM((256, 256), F32),
            pltpu.VMEM((2, 128, 128), F32),
            pltpu.VMEM((64, C4), BF16),
            pltpu.VMEM((2 * ngz, 64, C4), BF16),
            pltpu.VMEM((8, C4), BF16),
            pltpu.VMEM((ngz, 8, C4), BF16),
            pltpu.VMEM((3, 18, PLANE, C4), BF16),
            pltpu.VMEM((18, 48, C4), F32),
            pltpu.VMEM((2, 3, 2, 64, 128), BF16),
            pltpu.VMEM((2, 3, 2, 64, 128), BF16),
            pltpu.VMEM((2, 2, 64, 128), F32),
            pltpu.SemaphoreType.REGULAR,
            pltpu.SemaphoreType.DMA((5,)),
            pltpu.SemaphoreType.DMA((26,)),
            pltpu.SemaphoreType.DMA((26,)),
            pltpu.SemaphoreType.DMA,
            pltpu.SemaphoreType.DMA((2,)),
            pltpu.SemaphoreType.DMA,
            pltpu.SemaphoreType.DMA,
            pltpu.SemaphoreType.DMA((3,)),
            pltpu.SemaphoreType.DMA((3,)),
            pltpu.SemaphoreType.DMA((2,)),
            pltpu.SemaphoreType.DMA((2, 3)),
        ],
        compiler_params=pltpu.CompilerParams(
            collective_id=0, has_side_effects=True, vmem_limit_bytes=40 * 1024 * 1024
        ),
    )(
        *(pltpu.with_memory_space_constraint(x, pltpu.HBM) for x in (volume, conv4_weight.reshape(27 * CIN, C4), jnp.swapaxes(conv5_weight, 3, 4).reshape(3, 9, FILTERS, C4))),
    )
    cells = packed.reshape(4, 2, PLANE, 4, FILTERS).transpose(0, 3, 1, 2, 4)
    return cells.reshape(1, PLANE, PLANE, FILTERS)


def solution(mesh):
    sizes = (mesh.shape["gx"], mesh.shape["gy"], mesh.shape["gz"])
    return jax.shard_map(
        functools.partial(body, sizes),
        mesh=mesh,
        in_specs=(
            P(("sample", "gx"), "gy", "gz", None),
            P(),
            P(None, None, None, None, ("gy", "gz")),
        ),
        out_specs=P(("sample", "gx"), None, None, ("gy", "gz")),
        check_vma=False,
    )
```

```python
import functools

import jax
import jax.numpy as jnp
from jax import lax
from jax.experimental import pallas as pl
from jax.experimental.pallas import tpu as pltpu
from jax.sharding import PartitionSpec as P

MESH = pl.DeviceIdType.MESH
BF16, F32 = jnp.bfloat16, jnp.float32
CIN, C4, FILTERS = 128, 256, 32
PLANE = 32
SHIFTS = [(i, j, k) for i in (-1, 0, 1) for j in (-1, 0, 1) for k in (-1, 0, 1) if (i, j, k) != (0, 0, 0)]


def kernel(
    sizes, v, w4, w5, out,
    pad, wide, taps, w4b, w5b, zs, yz, zh, ch, hidden, early, late, pool, block, blocks, rim, rims, slab, broad, sent, got, packed,
    known, load_sem, halo_send, halo_recv, block_send, block_recv, rim_send, rim_recv, part_recv, shard_send, shard_recv,
):
    ngx, ngy, ngz = sizes
    g, a, b = lax.axis_index("gx"), lax.axis_index("gy"), lax.axis_index("gz")
    half = lax.div(a, 2)
    core = lax.rem(g, 2)
    other = ngy - 1 - a
    beside = 4 * half + 1 - a

    def there(dg, da, db):
        ok = None
        for at, step, n in ((g, dg, ngx), (a, da, ngy), (b, db, ngz)):
            if step:
                fine = (at > 0) if step < 0 else (at < n - 1)
                ok = fine if ok is None else jnp.logical_and(ok, fine)
        return ok

    def device(dg, da, db):
        return {"gx": g + dg, "gy": a + da, "gz": b + db}

    own_load = pltpu.make_async_copy(v, pad.at[1:3, 1:17], load_sem.at[0])
    own_load.start()
    w4_load = pltpu.make_async_copy(w4, w4b, load_sem.at[1])
    w4_load.start()
    w5_loads = [
        pltpu.make_async_copy(w5.at[dx], w5b.at[:, dx * FILTERS : (dx + 1) * FILTERS, :], load_sem.at[2 + dx]) for dx in range(3)
    ]
    for load in w5_loads:
        load.start()

    barrier = pltpu.get_barrier_semaphore()
    for shift in sorted(SHIFTS, key=lambda shift: -sum(map(abs, shift))):
        @pl.when(there(*shift))
        def _():
            pl.semaphore_signal(barrier, inc=1, device_id=device(*shift), device_id_type=MESH)
    pl.semaphore_signal(barrier, inc=1, device_id={"gy": other}, device_id_type=MESH)

    def near(position, n):
        return 1 + (position > 0).astype(jnp.int32) + (position < n - 1).astype(jnp.int32)

    greeted = near(g, ngx) * near(a, ngy) * near(b, ngz)

    def finish(stage):
        if stage < 2:
            w4_load.wait()
        if stage < 2:
            for load in w5_loads:
                load.wait()
        if stage == 2:
            halo_wait([shift for shift in SHIFTS if shift[0]])
            w4_load.wait()
        if 2 <= stage < 4:
            halo_sent()
            for piece in range(3):
                shard_copy(piece).wait_send()
                shard_copy(piece).wait_recv()
        if stage == 4:
            spread_sent()
        if stage >= 5:
            for k in range(3):
                @part_when(k, True)
                def _():
                    some_of(sent.at[1, 1] if k == 1 else sent.at[:, k], halo_send.at[k]).wait_send()

    yz[...] = jnp.zeros(yz.shape, F32)
    own_load.wait()
    for x in (1, 2):
        for y in range(1, 17):
            row = (x * 18 + y) * 32 + 8
            wide[row : row + 16, :] = pad[x, y].astype(F32)
    for side, z in ((0, 0), (1, 15)):
        for x in (0, 1):
            first = ((x + 1) * 18 + 1) * 32 + 8 + z
            column = wide[pl.ds(first, 16, stride=32), :]
            zs[side, x] = column.astype(BF16)
            for ys, y in ((0, 0), (1, 15)):
                yz[side, ys, x : x + 1, :] = column[y : y + 1]

    pl.semaphore_wait(barrier, greeted)

    def halo(shift):
        dg, da, db = shift
        x = {-1: 0, 1: 1}.get(dg)
        px = {-1: 3, 1: 0}.get(dg)
        y = {-1: 0, 1: 15}.get(da)
        py = {-1: 17, 1: 0}.get(da)
        s = {-1: 0, 1: 1}.get(db)
        if db == 0:
            if da == 0:
                src, dst = pad.at[x + 1, 1:17], pad.at[px, 1:17]
            elif dg == 0:
                src, dst = pad.at[1:3, y + 1], pad.at[1:3, py]
            else:
                src, dst = pad.at[x + 1, y + 1], pad.at[px, py]
        elif da == 0:
            if dg == 0:
                src, dst = zs.at[s], zh.at[1 - s, 1:3]
            else:
                src, dst = zs.at[s, x], zh.at[1 - s, px]
        else:
            ys = {-1: 0, 1: 1}[da]
            src, dst = yz.at[s, ys], ch.at[1 - s, 1 - ys, {-1: 2, 0: 1, 1: 0}[dg]]
        number = SHIFTS.index(shift)
        return pltpu.make_async_remote_copy(
            src_ref=src, dst_ref=dst, send_sem=halo_send.at[number], recv_sem=halo_recv.at[number],
            device_id=device(*shift), device_id_type=MESH,
        )

    def halo_sent():
        for shift in SHIFTS:
            @pl.when(there(*shift))
            def _():
                halo(shift).wait_send()

    def halo_wait(shifts):
        for shift in shifts:
            @pl.when(there(*(-i for i in shift)))
            def _():
                halo(shift).wait_recv()

    for shift in sorted(SHIFTS, key=lambda shift: (shift[0] != 0, -sum(map(abs, shift)))):
        @pl.when(there(*shift))
        def _():
            halo(shift).start()
    @pl.when(g == 0)
    def _():
        pad[0] = jnp.zeros(pad.shape[1:], BF16)
        zh[:, 0] = jnp.zeros((2, 16, CIN), BF16)
        ch[:, :, 0] = jnp.zeros((2, 2, 8, CIN), F32)

    @pl.when(g == ngx - 1)
    def _():
        pad[3] = jnp.zeros(pad.shape[1:], BF16)
        zh[:, 3] = jnp.zeros((2, 16, CIN), BF16)
        ch[:, :, 2] = jnp.zeros((2, 2, 8, CIN), F32)

    for side, edge_at in ((0, 0), (1, ngy - 1)):
        @pl.when(a == edge_at)
        def _():
            pad[:, 17 * side] = jnp.zeros((4, 16, CIN), BF16)
            ch[:, side] = jnp.zeros((2, 3, 8, CIN), F32)

    for side, edge_at in ((0, 0), (1, ngz - 1)):
        @pl.when(b == edge_at)
        def _():
            zh[side] = jnp.zeros((4, 16, CIN), BF16)
            ch[side] = jnp.zeros((2, 3, 8, CIN), F32)

    for dz in range(3):
        slab[dz, 17 * half] = jnp.zeros((PLANE, C4), BF16)
    broad[:, 0:8] = jnp.zeros((18, 8, C4), F32)
    broad[:, 40:48] = jnp.zeros((18, 8, C4), F32)


    def shard_rows(first, piece):
        return w5b.at[3 * piece : 3 * piece + 3, pl.ds(pl.multiple_of(first + 48 * core, 16), 48), :]

    def shard_copy(piece):
        return pltpu.make_async_remote_copy(
            src_ref=shard_rows(0, piece), dst_ref=shard_rows(96, piece),
            send_sem=shard_send.at[0], recv_sem=shard_recv.at[0, piece],
            device_id={"gy": other}, device_id_type=MESH,
        )

    def shard_relay(piece):
        return pltpu.make_async_remote_copy(
            src_ref=shard_rows(96, piece), dst_ref=shard_rows(96, piece),
            send_sem=shard_send.at[1], recv_sem=shard_recv.at[1, 0],
            device_id={"gx": g + 1 - 2 * core}, device_id_type=MESH,
        )

    for load in w5_loads:
        load.wait()
    for piece in range(3):
        shard_copy(piece).start()

    def widen(x):
        for y in range(18):
            if not (x in (1, 2) and 1 <= y <= 16):
                row = (x * 18 + y) * 32 + 8
                wide[row : row + 16, :] = pad[x, y].astype(F32)
        for side, at in ((0, 7), (1, 24)):
            wide[pl.ds((x * 18 + 1) * 32 + at, 16, stride=32), :] = zh[side, x].astype(F32)
            for ys, y in ((0, 0), (1, 17)):
                source, row = ((0, 1), (1, 0), (1, 1), (2, 0))[x]
                first = (x * 18 + y) * 32 + at
                wide[first : first + 1, :] = ch[side, ys, source, row : row + 1, :]
        for y in range(18):
            row = (x * 18 + y) * 32
            left = wide[row + 7 : row + 23, :].astype(BF16)
            right = wide[row + 9 : row + 25, :].astype(BF16)
            taps[x, y * 16 : y * 16 + 16, :] = jnp.concatenate([left, pad[x, y], right], axis=-1)

    def around(x):
        return jnp.concatenate([taps[x, dy * 16 : dy * 16 + 256, :] for dy in range(3)], axis=-1)

    halo_wait([shift for shift in SHIFTS if shift[0] == 0])
    for db in (-1, 1):
        @pl.when(there(0, 0, db))
        def _():
            pl.semaphore_signal(known, inc=1, device_id=device(0, 0, db), device_id_type=MESH)
    for x in (1, 2):
        widen(x)
    w4_load.wait()
    span = 9 * CIN
    own = jnp.concatenate([around(1), around(2)], axis=-1)
    for x in (0, 1):
        first = (1 - x) * span
        hidden[x] = jnp.dot(own, w4b[first : first + 2 * span, :], preferred_element_type=F32)
    halo_wait([shift for shift in SHIFTS if shift[0]])
    for x in (0, 3):
        widen(x)
    tops = jnp.maximum(
        hidden[0] + jnp.dot(around(0), w4b[:span, :], preferred_element_type=F32),
        hidden[1] + jnp.dot(around(3), w4b[2 * span :, :], preferred_element_type=F32),
    )
    tops = jnp.max(tops.reshape(8, 2, 16, C4), axis=1).reshape(128, C4)
    for lanes in range(2):
        pool[lanes] = tops[:, lanes * 128 : lanes * 128 + 128]
    for lanes in range(2):
        tops = jnp.maximum(pool[lanes, pl.ds(0, 64, stride=2), :], pool[lanes, pl.ds(1, 64, stride=2), :])
        block[:, lanes * 128 : lanes * 128 + 128] = jnp.where(tops > 0, tops, 0.3 * tops).astype(BF16)

    mine = (a - 2 * half) * ngz + b
    offsets = [(di, db) for di in range(2) for db in range(ngz) if (di, db) != (0, 0)]

    def spread(di, db):
        return pltpu.make_async_remote_copy(
            src_ref=block, dst_ref=blocks.at[mine], send_sem=block_send, recv_sem=block_recv.at[di],
            device_id={"gy": beside if di else a, "gz": lax.rem(b + db, ngz)}, device_id_type=MESH,
        )

    def some_of(ref, sem):
        return pltpu.make_async_remote_copy(
            src_ref=ref, dst_ref=ref, send_sem=sem, recv_sem=sem, device_id={"gz": lax.rem(b + 1, ngz)}, device_id_type=MESH
        )

    def rim_copy(t, db):
        return pltpu.make_async_remote_copy(
            src_ref=rim, dst_ref=rims.at[b], send_sem=rim_send, recv_sem=rim_recv,
            device_id={"gy": 2 * (1 - half) + t, "gz": lax.rem(b + db, ngz)}, device_id_type=MESH,
        )

    for at, first in ((1, 56), (2, 0)):
        @pl.when(a == at)
        def _():
            rim[...] = block[first : first + 8, :]

    pl.semaphore_wait(known, near(b, ngz) - 1)

    @pl.when(jnp.logical_or(a == 1, a == 2))
    def _():
        for db in (2, 1, 3, 0):
            for t in range(2):
                rim_copy(t, db).start()

    for di, db in ((1, 2), (0, 2), (1, 1), (1, 3), (0, 1), (0, 3), (1, 0)):
        spread(di, db).start()

    blocks[mine] = block[...]
    halo_sent()
    for piece in range(3):
        shard_copy(piece).wait_recv()
        shard_relay(piece).start()

    def spread_sent():
        for kind in range(2):
            some_of(w5b.at[:, 0:48], shard_send.at[kind]).wait_send()
        some_of(blocks.at[0:7], block_send).wait_send()

        @pl.when(jnp.logical_or(a == 1, a == 2))
        def _():
            some_of(block, rim_send).wait_send()

    def lay(first, rows):
        for dz in range(3):
            for row in range(rows):
                slab[dz, first + row] = broad[first + row, 7 + dz : 39 + dz, :].astype(BF16)

    at = a - 2 * half
    taps_w5 = (((1,), (1,)), ((), ()))

    def settle(di, row):
        some_of(blocks.at[pl.ds(4 * row, 4)] if di else blocks.at[0:3], block_recv.at[di]).wait_recv()
        for z in range(ngz):
            broad[pl.ds(1 + 8 * row, 8), 8 + 8 * z : 16 + 8 * z, :] = blocks[row * ngz + z].astype(F32).reshape(8, 8, C4)
        lay(1 + 8 * row, 8)

    def all_taps(numbers):
        return jnp.concatenate([w5b[number] for number in numbers], axis=-1)

    def rows_of(first, rows):
        return jnp.concatenate(
            [slab[dz, pl.ds(first + dy, rows)].reshape(rows * PLANE, C4) for dy in range(3) for dz in range(3)], axis=-1
        )

    settle(0, at)
    for dz in range(3):
        for row in (8 * at, 8 * at + 9):
            slab[dz, row] = jnp.zeros((PLANE, C4), BF16)
    some_of(w5b.at[:, 0:48], shard_recv.at[1, 0]).wait_recv()
    for part in range(2):
        early[128 * part : 128 * part + 128, :192] = lax.dot_general(
            rows_of(8 * at + 4 * part, 4), all_taps(range(9)), taps_w5, preferred_element_type=F32
        )
    settle(1, 1 - at)
    some_of(rims, rim_recv).wait_recv()
    for z in range(ngz):
        broad[17 * (1 - half), 8 + 8 * z : 16 + 8 * z, :] = rims[z].astype(F32)
    lay(17 * (1 - half), 1)

    parts = [(p, k) for p in (1, 0) for k in (0, 2, 1) if (p, k) != (0, 1)]

    def part_when(k, sender):
        if k == 1:
            return lambda f: f()
        if (k == 0) == sender:
            return pl.when(g < ngx - 1)
        return pl.when(g > 0)

    def part_copy(p, k, q):
        return pltpu.make_async_remote_copy(
            src_ref=sent.at[p, k, q], dst_ref=got.at[p, k, q], send_sem=halo_send.at[k], recv_sem=part_recv.at[k],
            device_id={"gx": g + 1 - k, "gy": other if p else a}, device_id_type=MESH,
        )

    lane = lax.broadcasted_iota(jnp.int32, (64, 128), 1)

    def group(rows, j):
        tile, k = divmod(j, 4)
        moved = [
            pltpu.roll(rows[64 * u : 64 * u + 64, 128 * tile : 128 * tile + 128], (32 * (u - k)) % 128, axis=1)
            if u != k else rows[64 * u : 64 * u + 64, 128 * tile : 128 * tile + 128]
            for u in range(4)
        ]
        return jnp.where(lane < 64, jnp.where(lane < 32, moved[0], moved[1]), jnp.where(lane < 96, moved[2], moved[3]))

    def send_parts(total, slot):
        for p, k in parts:
            sent[p, k, slot] = group(total, 3 * p + k).astype(BF16)

            @part_when(k, True)
            def _():
                part_copy(p, k, slot).start()

        packed[0, slot] = group(total, 1)

    for row, first, dy in ((8 * at, 0, 0), (8 * at + 9, 224, 2)):
        early[first : first + PLANE, :192] += lax.dot_general(
            jnp.concatenate([slab[dz, row] for dz in range(3)], axis=-1),
            all_taps(range(3 * dy, 3 * dy + 3)),
            taps_w5, preferred_element_type=F32,
        )
    send_parts(early[...], 0)
    for part in range(2):
        late[128 * part : 128 * part + 128, :192] = lax.dot_general(
            rows_of(8 * (1 - at) + 4 * part, 4), all_taps(range(9)), taps_w5, preferred_element_type=F32
        )
    send_parts(late[...], 1)

    spread_sent()
    some_of(got.at[1, 1], part_recv.at[1]).wait_recv()
    packed[1] = got[1, 1].astype(F32)
    for k in (0, 2):
        @part_when(k, False)
        def _():
            some_of(got.at[:, k], part_recv.at[k]).wait_recv()
            packed[...] += got[:, k].astype(F32)

    for p, place in ((0, half), (1, 1 - half)):
        for slot in range(2):
            out[place, at if p == slot else 1 - at] = packed[p, slot].astype(BF16)

    finish(9)


def body(sizes, volume, conv4_weight, conv5_weight):
    ngx, ngy, ngz = sizes
    any_space = pl.BlockSpec(memory_space=pl.ANY)
    packed = pl.pallas_call(
        functools.partial(kernel, sizes),
        out_shape=jax.ShapeDtypeStruct((2, 2, 64, 128), BF16),
        in_specs=[any_space] * 3,
        out_specs=pl.BlockSpec(memory_space=pltpu.VMEM),
        scratch_shapes=[
            pltpu.VMEM((4, 18, 16, CIN), BF16),
            pltpu.VMEM((4 * 18 * 32, CIN), F32),
            pltpu.VMEM((4, 18 * 16, 3 * CIN), BF16),
            pltpu.VMEM((27 * CIN, C4), BF16),
            pltpu.VMEM((9, 192, C4), BF16),
            pltpu.VMEM((2, 2, 16, CIN), BF16),
            pltpu.VMEM((2, 2, 8, CIN), F32),
            pltpu.VMEM((2, 4, 16, CIN), BF16),
            pltpu.VMEM((2, 2, 3, 8, CIN), F32),
            pltpu.VMEM((2, 256, C4), F32),
            pltpu.VMEM((256, 256), F32),
            pltpu.VMEM((256, 256), F32),
            pltpu.VMEM((2, 128, 128), F32),
            pltpu.VMEM((64, C4), BF16),
            pltpu.VMEM((2 * ngz, 64, C4), BF16),
            pltpu.VMEM((8, C4), BF16),
            pltpu.VMEM((ngz, 8, C4), BF16),
            pltpu.VMEM((3, 18, PLANE, C4), BF16),
            pltpu.VMEM((18, 48, C4), F32),
            pltpu.VMEM((2, 3, 2, 64, 128), BF16),
            pltpu.VMEM((2, 3, 2, 64, 128), BF16),
            pltpu.VMEM((2, 2, 64, 128), F32),
            pltpu.SemaphoreType.REGULAR,
            pltpu.SemaphoreType.DMA((5,)),
            pltpu.SemaphoreType.DMA((26,)),
            pltpu.SemaphoreType.DMA((26,)),
            pltpu.SemaphoreType.DMA,
            pltpu.SemaphoreType.DMA((2,)),
            pltpu.SemaphoreType.DMA,
            pltpu.SemaphoreType.DMA,
            pltpu.SemaphoreType.DMA((3,)),
            pltpu.SemaphoreType.DMA((2,)),
            pltpu.SemaphoreType.DMA((2, 3)),
        ],
        compiler_params=pltpu.CompilerParams(
            collective_id=0, has_side_effects=True, vmem_limit_bytes=40 * 1024 * 1024
        ),
    )(
        *(pltpu.with_memory_space_constraint(x, pltpu.HBM) for x in (volume, conv4_weight.reshape(27 * CIN, C4), jnp.swapaxes(conv5_weight, 3, 4).reshape(3, 9, FILTERS, C4))),
    )
    cells = packed.reshape(4, 2, PLANE, 4, FILTERS).transpose(0, 3, 1, 2, 4)
    return cells.reshape(1, PLANE, PLANE, FILTERS)


def solution(mesh):
    sizes = (mesh.shape["gx"], mesh.shape["gy"], mesh.shape["gz"])
    return jax.shard_map(
        functools.partial(body, sizes),
        mesh=mesh,
        in_specs=(
            P(("sample", "gx"), "gy", "gz", None),
            P(),
            P(None, None, None, None, ("gy", "gz")),
        ),
        out_specs=P(("sample", "gx"), None, None, ("gy", "gz")),
        check_vma=False,
    )
```
